32 devices in a mesh: row: 8 (over y, x, core), col: 4 (over z).
Axes of the slice: x: 2, y: 2, z: 4, core: 2. Of those that a mesh axis runs over, the one named last changes fastest.
Arguments:
- tokens: bfloat16 [128, 96, 768], P('row', 'col'), as said below
- dw_kernel: float32 [7, 7, 768], replicated, may hold values from -0.875 to 0.875
- norm_gain: float32 [768], replicated, may hold values from 0.5 to 1.5
- norm_shift: float32 [768], replicated, may hold values from -3 to 3
- w_in: bfloat16 [768, 3072], P(None, 'col'), may hold values from -0.21875 to 0.21875
- w_out: bfloat16 [3072, 768], P('col'), may hold values from -0.109375 to 0.109375
- w_kv: bfloat16 [768, 1536], P(None, 'col'), as said below
- queries: bfloat16 [512, 768], replicated, may hold values from -300 to 300, as said below
- latent_gain: float32 [768], replicated, may hold values from 0.5 to 1.5
- w_o: bfloat16 [768, 768], P(None, 'col'), may hold values from -0.21875 to 0.21875
Outputs:
- token_map: bfloat16 [128, 96, 768], P('row', 'col')
- latents: bfloat16 [512, 768], replicated
The draws below stay inside these ranges and needn't reach their ends.
Inputs may be any that keep to these rules, and one draw needn't show every extreme that they name: Latent queries; a few rows may be far larger than the others. `tokens`: patch token features, roughly unit normal, between -24 and 24; a few cells hold 24 in two channels. `w_kv`: key and value projection weights.
All inputs are finite; a program needn't handle non-finite values.
Results may differ from the reference program's by a relative error of at most 0.011.
Values may be sent and summed in bfloat16 or wider, within the bound.
A program may use at most 64 MiB of HBM per device.

```python
import math
import jax
import jax.numpy as jnp
from jax import lax

D = 768
FF = 3072
HEADS = 12
HEAD = 64
LATENTS = 512
HD = 16
WD = 24
H = 128
W = 96


def kv_matrix(key):
    values = jax.random.normal(jax.random.fold_in(key, 21), (D, 2 * D), jnp.float32)
    return jnp.clip(values, -6.0, 6.0) / jnp.sqrt(jnp.float32(D))


def channel_pairs():
    latent_ids = jnp.arange(LATENTS, dtype=jnp.int32)
    first = latent_ids % D
    second = (first + 1 + latent_ids // D) % D
    return (latent_ids, first, second)


def draw_w_kv(key, part):
    return kv_matrix(key).astype(jnp.bfloat16)


def draw_tokens(key, part):
    base = jax.random.normal(jax.random.fold_in(key, 31), (H, W, D), jnp.float32)
    base = jnp.clip(base, -6.0, 6.0)
    latent_ids, first, second = channel_pairs()
    grid_cols = W // WD
    device_count = H // HD * grid_cols
    per_device = LATENTS // device_count
    owner = latent_ids // per_device
    target = (owner + device_count // 2) % device_count
    slot = latent_ids % per_device
    row_pos = target // grid_cols * HD + slot // WD
    col_pos = target % grid_cols * WD + slot % WD
    base = base.at[row_pos, col_pos, first].set(24.0)
    base = base.at[row_pos, col_pos, second].set(24.0)
    return base.astype(jnp.bfloat16)


def draw_queries(key, part):
    matrix = kv_matrix(key)
    latent_ids, first, second = channel_pairs()
    aligned = 48.0 * (matrix[first, :D] + matrix[second, :D])
    noise = jnp.clip(jax.random.normal(jax.random.fold_in(key, 11), (LATENTS, D), jnp.float32), -5.0, 5.0)
    values = aligned + 0.5 * noise
    return values.astype(jnp.bfloat16)


def block_levels(own_key, shape, cuts, least, top_value):
    def one(dim, blocks):
        heights = jax.random.uniform(jax.random.fold_in(jax.random.fold_in(own_key, 6), dim), (blocks,), jnp.float32, least / len(cuts), top_value / len(cuts))
        return jnp.repeat(jnp.exp(heights), shape[dim] // blocks).reshape((-1,) + (1,) * (len(shape) - dim - 1))

    factor_of = one(*cuts[0])
    for cut in cuts[1:]:
        factor_of = factor_of * one(*cut)
    return factor_of


def gaussian(key, extent, deviation, limit, split=(), kind=jnp.bfloat16):
    array = jax.random.normal(key, extent, jnp.float32) * deviation
    if len(split) > 0:
        array = block_levels(key, extent, split, -0.22, 0.18) * array
    return jnp.clip(array, min=-limit, max=limit).astype(kind)


def setup_inputs(seed: int = 0) -> dict:
    splits = jax.random.split(jax.random.key(seed), 11)
    tokens = draw_tokens(jax.random.fold_in(splits[10], 71), 0)
    dw_kernel = gaussian(splits[1], (7, 7, D), 49 ** -0.5, 0.875, (), jnp.float32)
    norm_gain = jnp.clip(1.0 + 0.1 * jax.random.normal(splits[2], (D,), jnp.float32), 0.5, 1.5)
    norm_shift = gaussian(splits[3], (D,), 0.5, 3.0, (), jnp.float32)
    w_in = gaussian(splits[4], (D, FF), D ** -0.5, 0.21875, ((1, 4),))
    w_out = gaussian(splits[5], (FF, D), FF ** -0.5, 0.109375, ((0, 4),))
    w_kv = draw_w_kv(jax.random.fold_in(splits[10], 71), 0)
    queries = draw_queries(jax.random.fold_in(splits[10], 71), 0)
    latent_gain = jnp.clip(1.0 + 0.1 * jax.random.normal(splits[8], (D,), jnp.float32), 0.5, 1.5)
    w_o = gaussian(splits[9], (D, D), D ** -0.5, 0.21875, ((1, 4),))
    return {"tokens": tokens, "dw_kernel": dw_kernel, "norm_gain": norm_gain, "norm_shift": norm_shift, "w_in": w_in, "w_out": w_out, "w_kv": w_kv, "queries": queries, "latent_gain": latent_gain, "w_o": w_o}


def conv_taps(padded, height, width, dw_kernel):
    mixed = jnp.zeros((height, width, padded.shape[2]), jnp.float32)
    for row_tap in range(7):
        for col_tap in range(7):
            mixed = mixed + padded[row_tap:row_tap + height, col_tap:col_tap + width] * dw_kernel[row_tap, col_tap]
    return mixed

def layer_norm(mixed, norm_gain, norm_shift):
    center = mixed - lax.optimization_barrier(jnp.mean(mixed, axis=-1, keepdims=True))
    spread = lax.optimization_barrier(jnp.mean(center * center, axis=-1, keepdims=True))
    return (center * lax.rsqrt(spread + 1e-06) * norm_gain + norm_shift).astype(jnp.bfloat16)

def finish_latents(numer, denom, latent_gain, w_o):
    attended = (numer / denom[..., None]).reshape(numer.shape[0], -1)
    squares = lax.optimization_barrier(jnp.mean(attended * attended, axis=-1, keepdims=True))
    scaled = (attended * lax.rsqrt(squares + 1e-06) * latent_gain).astype(jnp.bfloat16)
    return jnp.dot(scaled, w_o, preferred_element_type=jnp.float32).astype(jnp.bfloat16)

def reference(tokens, dw_kernel, norm_gain, norm_shift, w_in, w_out, w_kv, queries, latent_gain, w_o):
    padded = jnp.pad(tokens.astype(jnp.float32), ((3, 3), (3, 3), (0, 0)))
    mixed = conv_taps(padded, H, W, dw_kernel)
    normed = layer_norm(mixed, norm_gain, norm_shift)
    block_rows = math.gcd(H * W, 4096)
    count = H * W // block_rows
    normed_blocks = normed.reshape(count, block_rows, D)
    token_blocks = tokens.reshape(count, block_rows, D)

    def mlp_block(pair):
        normed_rows, token_rows = pair
        hidden = jax.nn.gelu(jnp.dot(normed_rows, w_in, preferred_element_type=jnp.float32)).astype(jnp.bfloat16)
        update = jnp.dot(hidden, w_out, preferred_element_type=jnp.float32)
        output = (token_rows.astype(jnp.float32) + update).astype(jnp.bfloat16)
        keys_vals = jnp.dot(output, w_kv, preferred_element_type=jnp.float32).astype(jnp.bfloat16)
        return (output, keys_vals)
    out_blocks, kv_blocks = lax.map(mlp_block, (normed_blocks, token_blocks))
    token_map = out_blocks.reshape(H, W, D)
    query_heads = queries.astype(jnp.float32).reshape(LATENTS, HEADS, HEAD)
    score_scale = 1.0 / math.sqrt(HEAD)

    def block_scores(kv_block):
        key_heads = kv_block[:, :D].astype(jnp.float32).reshape(-1, HEADS, HEAD)
        return jnp.einsum('lhd,thd->lht', query_heads, key_heads, precision=lax.Precision.HIGHEST) * score_scale

    def block_max(kv_block):
        return lax.optimization_barrier(jnp.max(block_scores(kv_block), axis=-1))
    maxima = lax.optimization_barrier(jnp.max(lax.map(block_max, kv_blocks), axis=0))

    def accumulate(running, kv_block):
        denom, numer = running
        weights = jnp.exp(block_scores(kv_block) - maxima[..., None])
        denom = denom + lax.optimization_barrier(jnp.sum(weights, axis=-1))
        rounded = lax.optimization_barrier(weights.astype(jnp.bfloat16)).astype(jnp.float32)
        val_heads = kv_block[:, D:].astype(jnp.float32).reshape(-1, HEADS, HEAD)
        numer = numer + jnp.einsum('lht,thd->lhd', rounded, val_heads, precision=lax.Precision.HIGHEST)
        return ((denom, numer), None)
    start = (jnp.zeros((LATENTS, HEADS), jnp.float32), jnp.zeros((LATENTS, HEADS, HEAD), jnp.float32))
    (denom, numer), unused = lax.scan(accumulate, start, kv_blocks)
    latents = finish_latents(numer, denom, latent_gain, w_o)
    return (token_map, latents)
```

```python
import functools
import math

import jax
import jax.numpy as jnp
from jax import lax
from jax.experimental import pallas as pl
from jax.experimental.pallas import tpu as pltpu
from jax.sharding import PartitionSpec as P

HEADS = 12
HEAD = 64
HALO = 3
EDGE = 8
LANES = 128
MESH = pl.DeviceIdType.MESH
VMEM_BYTES = 60 * 1024 * 1024


def log2(count):
    return count.bit_length() - 1


def barrier_with(peers):
    barrier = pltpu.get_barrier_semaphore()
    total = 0
    for cond, device in peers:
        if cond is None:
            pl.semaphore_signal(barrier, inc=1, device_id=device, device_id_type=MESH)
            total = total + 1
        else:

            @pl.when(cond)
            def _():
                pl.semaphore_signal(barrier, inc=1, device_id=device, device_id_type=MESH)

            total = total + jnp.where(cond, 1, 0)
    pl.semaphore_wait(barrier, total)


def block_kernel(
    rows,
    cols,
    tokens,
    left_edge,
    right_edge,
    dw,
    gain,
    shift,
    w_in,
    w_out,
    w_kv,
    w_o,
    queries,
    tok_out,
    num_out,
    stat_out,
    wo_out,
    g_in,
    g_out,
    g_kv,
    pad,
    mixed,
    normed,
    hidden,
    acc,
    tok_bf,
    kv,
    h_rows,
    h_cols,
    h_corners,
    halo_send,
    halo_recv,
    send_sem,
    recv_sem,
    local_sem,
):
    bits = log2(rows)
    row, col = lax.axis_index("row"), lax.axis_index("col")
    height, width, depth = tokens.shape
    count = height * width
    coords = [(row // (1 << (bits - 1 - i))) % 2 for i in range(bits)]

    def partner(dim):
        step = 1 << (bits - 1 - dim)
        return row + step * (1 - 2 * coords[dim])

    halo = []
    for dr in (-1, 0, 1):
        for dc in (-1, 0, 1):
            if dr == 0 and dc == 0:
                continue
            cond = None
            for d, pos, n in ((dr, row, rows), (dc, col, cols)):
                if d:
                    one = (pos + d >= 0) & (pos + d < n)
                    cond = one if cond is None else cond & one
            halo.append((dr, dc, cond))

    peers = [(cond, (row + dr, col + dc)) for dr, dc, cond in halo]
    peers += [(None, (row, (col + j) % cols)) for j in range(1, cols)]
    peers += [(None, (partner(i), col)) for i in range(bits)]
    barrier_with(peers)

    def halo_slot(dr, dc):
        if dc == 0:
            return h_rows.at[0 if dr < 0 else 1]
        if dr == 0:
            return h_cols.at[0 if dc < 0 else 1]
        return h_corners.at[(0 if dr < 0 else 2) + (0 if dc < 0 else 1)]

    def halo_copy(i, dr, dc):
        edge = tokens if dc == 0 else (left_edge if dc < 0 else right_edge)
        if dr == 0:
            src = edge
        elif dr < 0:
            src = edge.at[pl.ds(0, HALO)]
        else:
            src = edge.at[pl.ds(height - HALO, HALO)]
        return pltpu.make_async_remote_copy(
            src_ref=src,
            dst_ref=halo_slot(-dr, -dc),
            send_sem=halo_send.at[i],
            recv_sem=halo_recv.at[len(halo) - 1 - i],
            device_id=(row + dr, col + dc),
            device_id_type=MESH,
        )

    for i, (dr, dc, cond) in enumerate(halo):

        @pl.when(cond)
        def _():
            halo_copy(i, dr, dc).start()

    shards = (w_in, w_out, w_kv, w_o)
    fulls = (g_in, g_out, g_kv, wo_out)
    units = [(w, j) for w in range(4) for j in range(1, cols)]
    own = tuple(coords)

    def unit_copy(u, phase):
        w, j = units[u]
        if phase == 0:
            target = (row, (col + cols - j) % cols)
            src = shards[w].at[own]
            dst = fulls[w].at[(col,) + own]
        else:
            order = list(range(bits - 1))
            if u % 2:
                order = order[::-1]
            order = order + [bits - 1]
            done = order[: phase - 1]
            block = (col + j) % cols
            idx = (block,) + tuple(slice(None) if i in done else own[i] for i in range(bits))
            src = fulls[w].at[idx]
            dst = fulls[w].at[idx]
            target = (partner(order[phase - 1]), col)
        slot = u * (bits + 1) + phase
        return pltpu.make_async_remote_copy(
            src_ref=src,
            dst_ref=dst,
            send_sem=send_sem.at[slot],
            recv_sem=recv_sem.at[slot],
            device_id=target,
            device_id_type=MESH,
        )

    for u in range(len(units)):
        unit_copy(u, 0).start()
    local = []
    for w in range(4):
        copy = pltpu.make_async_copy(shards[w], fulls[w].at[col], local_sem.at[w])
        copy.start()
        local.append(copy)

    state = {"tick": 0}
    ticks = len(units) + bits

    def tick():
        t = state["tick"]
        if t >= ticks:
            return
        state["tick"] = t + 1
        for phase in range(bits, -1, -1):
            u = t - phase
            if 0 <= u < len(units):
                unit_copy(u, phase).wait_recv()
                if phase < bits:
                    unit_copy(u, phase + 1).start()

    def finish_unit(u):
        while state["tick"] <= u + bits:
            tick()

    pad[pl.ds(HALO, height), pl.ds(EDGE, width), :] = tokens[...].astype(jnp.float32)
    spans = {-1: (0, HALO), 0: (HALO, height), 1: (HALO + height, HALO)}
    lanes_of = {-1: (0, EDGE), 0: (EDGE, width), 1: (EDGE + width, EDGE)}
    for i, (dr, dc, cond) in enumerate(halo):
        r0, rn = spans[dr]
        c0, cn = lanes_of[dc]

        @pl.when(cond)
        def _():
            halo_copy(len(halo) - 1 - i, -dr, -dc).wait_recv()
            pad[pl.ds(r0, rn), pl.ds(c0, cn), :] = halo_slot(dr, dc)[...].astype(jnp.float32)

        @pl.when(jnp.logical_not(cond))
        def _():
            pad[pl.ds(r0, rn), pl.ds(c0, cn), :] = jnp.zeros((rn, cn, depth), jnp.float32)

    taps = 2 * HALO + 1
    chunks = depth // LANES

    def conv_rows(first, n_rows):
        def one(step, carry):
            i = first + step // chunks
            q = pl.multiple_of((step % chunks) * LANES, LANES)
            sums = [None] * taps
            for a in range(taps):
                line = pad[i + a, :, pl.ds(q, LANES)]
                for b in range(taps):
                    lo = 0 if b < HALO else EDGE
                    hi = EDGE + width + (EDGE if b > HALO else 0)
                    term = line[lo:hi] * dw[a, pl.ds(b, 1), pl.ds(q, LANES)]
                    sums[b] = term if sums[b] is None else sums[b] + term
            total = sums[HALO]
            for b in range(taps):
                if b == HALO:
                    continue
                size = width + EDGE
                offset = EDGE - HALO + b - (0 if b < HALO else EDGE)
                total = total + pltpu.roll(sums[b], (size - offset) % size, 0)[:width]
            mixed[i, :, pl.ds(q, LANES)] = total
            return carry

        lax.fori_loop(0, n_rows * chunks, one, 0)

    group = 2
    span = group * width

    def norm_rows(g, carry):
        value = mixed[pl.ds(g * group, group), :, :].reshape(span, depth)
        center = value - jnp.mean(value, axis=-1, keepdims=True)
        spread = jnp.mean(center * center, axis=-1, keepdims=True)
        out = center * lax.rsqrt(spread + 1e-06) * gain[...] + shift[...]
        normed[pl.ds(pl.multiple_of(g * span, 16), span), :] = out.astype(jnp.bfloat16)
        return carry

    quarter = height // 4
    for part in range(4):
        conv_rows(part * quarter, quarter)
        tick()
    lax.fori_loop(0, height // group, norm_rows, 0)
    for copy in local:
        copy.wait()

    def wide(ref, block, lo, size):
        value = ref[(block,) + (slice(None),) * (bits + 1) + (pl.ds(lo, size),)]
        return value.reshape(-1, size)

    f_width = w_in.shape[-1]
    tile = 256 if f_width % 256 == 0 else LANES

    def expand(block):
        def one(n, carry):
            lo = pl.multiple_of(n * tile, tile)
            u = jnp.dot(normed[...], wide(g_in, block, lo, tile), preferred_element_type=jnp.float32)
            hidden[block, :, pl.ds(lo, tile)] = jax.nn.gelu(u).astype(jnp.bfloat16)
            return carry

        lax.fori_loop(0, f_width // tile, one, 0)

    def contract(block, fresh):
        def one(n, carry):
            lo = pl.multiple_of(n * 256, 256)
            part = jnp.dot(
                hidden[block], wide(g_out, block, lo, 256), preferred_element_type=jnp.float32
            )
            if fresh:
                acc[:, pl.ds(lo, 256)] = part
            else:
                acc[:, pl.ds(lo, 256)] += part
            return carry

        lax.fori_loop(0, depth // 256, one, 0)

    expand(col)
    tick()
    contract(col, True)
    for j in range(1, cols):
        finish_unit(j - 1)
        expand((col + j) % cols)
    for j in range(1, cols):
        finish_unit(cols - 1 + j - 1)
        contract((col + j) % cols, False)

    def close_rows(g, carry):
        base = pad[pl.ds(HALO + g * group, group), pl.ds(EDGE, width), :].reshape(span, depth)
        at = pl.ds(pl.multiple_of(g * span, 16), span)
        total = base + acc[at, :]
        tok_out[pl.ds(g * group, group), :, :] = total.reshape(group, width, depth).astype(jnp.bfloat16)
        tok_bf[at, :] = total.astype(jnp.bfloat16)
        return carry

    lax.fori_loop(0, height // group, close_rows, 0)

    kv_width = w_kv.shape[-1]

    def project(block):
        def one(n, carry):
            lo = pl.multiple_of(n * LANES, LANES)
            out = jnp.dot(tok_bf[...], wide(g_kv, block, lo, LANES), preferred_element_type=jnp.float32)
            kv[block, :, pl.ds(lo, LANES)] = out.astype(jnp.bfloat16)
            return carry

        lax.fori_loop(0, kv_width // LANES, one, 0)

    project(col)
    for j in range(1, cols):
        finish_unit(2 * (cols - 1) + j - 1)
        project((col + j) % cols)

    latents = queries.shape[0]
    scale = 1.0 / math.sqrt(HEAD)
    stat_out[...] = jnp.zeros((latents, LANES), jnp.float32)
    side = lax.broadcasted_iota(jnp.int32, (1, LANES), 1)

    def attend(pair, carry):
        at = pl.multiple_of(pair * LANES, LANES)
        k_at, v_at = at, depth + at
        keys = kv[k_at // kv_width, :, pl.ds(pl.multiple_of(k_at % kv_width, LANES), LANES)]
        vals = kv[v_at // kv_width, :, pl.ds(pl.multiple_of(v_at % kv_width, LANES), LANES)]
        q = queries[:, pl.ds(at, LANES)]
        stat = stat_out[...]
        outs = []
        for s in range(2):
            keep = (side // HEAD) == s
            q_one = jnp.where(keep, q, jnp.zeros_like(q))
            scores = lax.dot_general(
                q_one, keys, (((1,), (1,)), ((), ())), preferred_element_type=jnp.float32
            )
            top = jnp.max(scores, axis=-1, keepdims=True)
            weights = jnp.exp((scores - top) * scale)
            den = jnp.sum(weights, axis=-1, keepdims=True)
            outs.append(
                jnp.dot(weights.astype(jnp.bfloat16), vals, preferred_element_type=jnp.float32)
            )
            lane = pair * 2 + s
            stat = jnp.where(side == lane, top * scale, stat)
            stat = jnp.where(side == lane + HEAD, den, stat)
        stat_out[...] = stat
        num_out[:, pl.ds(at, LANES)] = jnp.where(side < HEAD, outs[0], outs[1]).astype(jnp.bfloat16)
        return carry

    lax.fori_loop(0, depth // LANES, attend, 0)

    finish_unit(len(units) - 1)
    for i, (dr, dc, cond) in enumerate(halo):

        @pl.when(cond)
        def _():
            halo_copy(i, dr, dc).wait_send()

    for u in range(len(units)):
        for phase in range(bits + 1):
            unit_copy(u, phase).wait_send()


def per_head(factors, n):
    side = lax.broadcasted_iota(jnp.int32, (1, LANES), 1)
    parts = []
    for pair in range(HEADS // 2):
        lo = jnp.broadcast_to(factors[:, 2 * pair : 2 * pair + 1], (n, LANES))
        hi = jnp.broadcast_to(factors[:, 2 * pair + 1 : 2 * pair + 2], (n, LANES))
        parts.append(jnp.where(side < HEAD, lo, hi))
    return jnp.concatenate(parts, axis=-1)


def merge(stats, nums):
    n = stats[0].shape[0]
    side = lax.broadcasted_iota(jnp.int32, (1, LANES), 1)
    peak = functools.reduce(jnp.maximum, stats)
    den, num = None, None
    for stat, part in zip(stats, nums):
        factor = jnp.exp(stat - peak)
        d = pltpu.roll(stat, HEAD, 1) * factor
        t = part.astype(jnp.float32) * per_head(factor, n)
        den = d if den is None else den + d
        num = t if num is None else num + t
    return jnp.where(side < HEAD, peak, pltpu.roll(den, HEAD, 1)), num


def latent_kernel(
    rows, cols, num_in, stat_in, latent_gain, out, num, stat, got_num, got_stat, send_sem, recv_sem
):
    bits = log2(rows)
    row, col = lax.axis_index("row"), lax.axis_index("col")
    latents = num_in.shape[0]

    def bit(i):
        return (row // (1 << i)) % 2

    def partner(i):
        return row + (1 << i) * (1 - 2 * bit(i))

    peers = [(None, (row, (col + j) % cols)) for j in range(1, cols)]
    peers += [(None, (partner(i), col)) for i in range(bits)]
    barrier_with(peers)

    def copy(src, dst, slot, device):
        return pltpu.make_async_remote_copy(
            src_ref=src,
            dst_ref=dst,
            send_sem=send_sem.at[slot],
            recv_sem=recv_sem.at[slot],
            device_id=device,
            device_id_type=MESH,
        )

    slot = 0
    sent = []
    base = 0
    size = latents
    offset = 0
    bases = []
    for i in range(bits):
        half = size // 2
        mine = base + bit(i) * half
        theirs = base + (1 - bit(i)) * half
        src_num, src_stat = (num_in, stat_in) if i == 0 else (num, stat)
        give = pl.ds(pl.multiple_of(theirs, 16), half)
        land = pl.ds(offset, half)
        pair = [
            copy(src_stat.at[give], got_stat.at[land], slot, (partner(i), col)),
            copy(src_num.at[give], got_num.at[land], slot + 1, (partner(i), col)),
        ]
        slot += 2
        for c in pair:
            c.start()
        for c in pair:
            c.wait_recv()
        sent += pair
        step = min(half, 32)

        def fold(k, carry):
            at = pl.ds(pl.multiple_of(mine + k * step, 16), step)
            came = pl.ds(pl.multiple_of(offset + k * step, 16), step)
            new_stat, new_num = merge(
                [src_stat[at, :], got_stat[came, :]], [src_num[at, :], got_num[came, :]]
            )
            stat[at, :] = new_stat
            num[at, :] = new_num.astype(jnp.bfloat16)
            return carry

        lax.fori_loop(0, half // step, fold, 0)
        bases.append((base, size))
        base, size, offset = mine, half, offset + half

    share = size // cols
    arrived = []
    for j in range(1, cols):
        other = (col + cols - j) % cols
        give = pl.ds(pl.multiple_of(base + other * share, 16), share)
        land = pl.ds(offset + (j - 1) * share, share)
        pair = [
            copy(stat.at[give], got_stat.at[land], slot, (row, other)),
            copy(num.at[give], got_num.at[land], slot + 1, (row, other)),
        ]
        slot += 2
        for c in pair:
            c.start()
        sent += pair
        arrived.append((pair, land))
    for pair, _ in arrived:
        for c in pair:
            c.wait_recv()
    own = pl.ds(pl.multiple_of(base + col * share, 16), share)
    final_stat, final_num = merge(
        [stat[own, :]] + [got_stat[land, :] for _, land in arrived],
        [num[own, :]] + [got_num[land, :] for _, land in arrived],
    )
    attended = final_num / per_head(pltpu.roll(final_stat, HEAD, 1), share)
    squares = jnp.mean(attended * attended, axis=-1, keepdims=True)
    scaled = attended * lax.rsqrt(squares + 1e-06) * latent_gain[...]
    out[own, :] = scaled.astype(jnp.bfloat16)

    gather = []
    for j in range(1, cols):
        c = copy(out.at[own], out.at[own], slot, (row, (col + cols - j) % cols))
        slot += 1
        c.start()
        gather.append(c)
    for c in gather:
        c.wait_recv()
    sent += gather
    for i in reversed(range(bits)):
        held = pl.ds(pl.multiple_of(base, 16), size)
        c = copy(out.at[held], out.at[held], slot, (partner(i), col))
        slot += 1
        c.start()
        c.wait_recv()
        sent.append(c)
        base, size = bases[i]
    for c in sent:
        c.wait_send()


def vmem(n):
    return [pl.BlockSpec(memory_space=pltpu.VMEM)] * n


def fits(mesh_rows, mesh_cols, tokens, w_in, w_kv, queries):
    height, width, depth = tokens.shape
    return (
        mesh_rows >= 2
        and mesh_cols >= 2
        and mesh_rows & (mesh_rows - 1) == 0
        and depth % (16 * mesh_rows) == 0
        and w_in.shape[1] % LANES == 0
        and w_kv.shape[1] % LANES == 0
        and queries.shape[0] % (16 * mesh_rows * mesh_cols) == 0
        and depth % 256 == 0
        and height % 4 == 0
        and width % 8 == 0
        and 2 * width % 16 == 0
    )


def kernel_body(tokens, dw_kernel, norm_gain, norm_shift, w_in, w_out, w_kv, queries, latent_gain, w_o):
    rows, cols = lax.axis_size("row"), lax.axis_size("col")
    height, width, depth = tokens.shape
    if not fits(rows, cols, tokens, w_in, w_kv, queries):
        return body(
            tokens, dw_kernel, norm_gain, norm_shift, w_in, w_out, w_kv, queries, latent_gain, w_o
        )
    bits = log2(rows)
    count = height * width
    latents = queries.shape[0]
    f_width = w_in.shape[1]
    grid = (2,) * bits
    bf16, f32 = jnp.bfloat16, jnp.float32

    def cut(w):
        return w.reshape(grid + (w.shape[0] // rows, w.shape[1]))

    shards = [cut(w) for w in (w_in, w_out, w_kv, w_o)]
    units = 4 * (cols - 1)
    token_map, num, stat, wo_full = pl.pallas_call(
        functools.partial(block_kernel, rows, cols),
        out_shape=(
            jax.ShapeDtypeStruct(tokens.shape, bf16),
            jax.ShapeDtypeStruct((latents, depth), bf16),
            jax.ShapeDtypeStruct((latents, LANES), f32),
            jax.ShapeDtypeStruct((cols,) + shards[3].shape, bf16),
        ),
        in_specs=vmem(11),
        out_specs=tuple(vmem(4)),
        scratch_shapes=[
            pltpu.VMEM((cols,) + shards[0].shape, bf16),
            pltpu.VMEM((cols,) + shards[1].shape, bf16),
            pltpu.VMEM((cols,) + shards[2].shape, bf16),
            pltpu.VMEM((height + 2 * HALO, width + 2 * EDGE, depth), f32),
            pltpu.VMEM((height, width, depth), f32),
            pltpu.VMEM((count, depth), bf16),
            pltpu.VMEM((cols, count, f_width), bf16),
            pltpu.VMEM((count, depth), f32),
            pltpu.VMEM((count, depth), bf16),
            pltpu.VMEM((cols, count, w_kv.shape[1]), bf16),
            pltpu.VMEM((2, HALO, width, depth), bf16),
            pltpu.VMEM((2, height, EDGE, depth), bf16),
            pltpu.VMEM((4, HALO, EDGE, depth), bf16),
            pltpu.SemaphoreType.DMA((8,)),
            pltpu.SemaphoreType.DMA((8,)),
            pltpu.SemaphoreType.DMA((units * (bits + 1),)),
            pltpu.SemaphoreType.DMA((units * (bits + 1),)),
            pltpu.SemaphoreType.DMA((4,)),
        ],
        compiler_params=pltpu.CompilerParams(
            collective_id=0, has_side_effects=True, vmem_limit_bytes=VMEM_BYTES
        ),
        name="block",
    )(
        tokens,
        tokens[:, :EDGE],
        tokens[:, width - EDGE :],
        dw_kernel,
        norm_gain.reshape(1, depth),
        norm_shift.reshape(1, depth),
        *shards,
        queries,
    )
    slots = 2 * bits + 3 * (cols - 1) + bits
    scaled = pl.pallas_call(
        functools.partial(latent_kernel, rows, cols),
        out_shape=jax.ShapeDtypeStruct((latents, depth), bf16),
        in_specs=vmem(3),
        out_specs=vmem(1)[0],
        scratch_shapes=[
            pltpu.VMEM((latents, depth), bf16),
            pltpu.VMEM((latents, LANES), f32),
            pltpu.VMEM((latents, depth), bf16),
            pltpu.VMEM((latents, LANES), f32),
            pltpu.SemaphoreType.DMA((slots,)),
            pltpu.SemaphoreType.DMA((slots,)),
        ],
        compiler_params=pltpu.CompilerParams(
            collective_id=1, has_side_effects=True, vmem_limit_bytes=VMEM_BYTES
        ),
        name="latents",
    )(num, stat, latent_gain.reshape(1, depth))
    w_full = wo_full.reshape(cols, depth, -1).transpose(1, 0, 2).reshape(depth, -1)
    latents_out = jnp.dot(scaled, w_full, preferred_element_type=f32).astype(bf16)
    return (token_map, latents_out)


def with_halo(cells, sides, width):
    for axis, dim in sides:
        count = lax.axis_size(axis)
        ends = count - 1
        head = lax.slice_in_dim(cells, 0, width, axis=dim)
        tail = lax.slice_in_dim(cells, cells.shape[dim] - width, cells.shape[dim], axis=dim)
        cells = jnp.concatenate(
            [
                lax.ppermute(tail, axis, [(i, (i + 1) % count) for i in range(ends)]),
                cells,
                lax.ppermute(head, axis, [((i + 1) % count, i) for i in range(ends)]),
            ],
            axis=dim,
        )
    return cells


def conv_taps(padded, height, width, dw_kernel):
    mixed = jnp.zeros((height, width, padded.shape[2]), jnp.float32)
    for row_tap in range(7):
        for col_tap in range(7):
            mixed = (
                mixed
                + padded[row_tap : row_tap + height, col_tap : col_tap + width]
                * dw_kernel[row_tap, col_tap]
            )
    return mixed


def layer_norm(mixed, norm_gain, norm_shift):
    center = mixed - jnp.mean(mixed, axis=-1, keepdims=True)
    spread = jnp.mean(center * center, axis=-1, keepdims=True)
    return (center * lax.rsqrt(spread + 1e-06) * norm_gain + norm_shift).astype(jnp.bfloat16)


def finish_latents(numer, denom, latent_gain, w_full):
    attended = (numer / denom[..., None]).reshape(numer.shape[0], -1)
    squares = jnp.mean(attended * attended, axis=-1, keepdims=True)
    scaled = (attended * lax.rsqrt(squares + 1e-06) * latent_gain).astype(jnp.bfloat16)
    return jnp.dot(scaled, w_full, preferred_element_type=jnp.float32).astype(jnp.bfloat16)


def body(tokens, dw_kernel, norm_gain, norm_shift, w_in, w_out, w_kv, queries, latent_gain, w_o):
    height, width, width_d = tokens.shape
    latent_count = queries.shape[0]
    padded = with_halo(tokens, (("row", 0), ("col", 1)), 3)
    mixed = conv_taps(padded.astype(jnp.float32), height, width, dw_kernel)
    normed = layer_norm(mixed, norm_gain, norm_shift).reshape(height * width, width_d)
    residual = tokens.reshape(height * width, width_d).astype(jnp.float32)
    hidden = jax.nn.gelu(
        jnp.dot(
            normed,
            lax.all_gather(w_in, "col", axis=1, tiled=True),
            preferred_element_type=jnp.float32,
        )
    ).astype(jnp.bfloat16)
    update = jnp.dot(
        hidden, lax.all_gather(w_out, "col", axis=0, tiled=True), preferred_element_type=jnp.float32
    )
    token_rows = (residual + update).astype(jnp.bfloat16)
    token_map = token_rows.reshape(height, width, width_d)
    keys_vals = jnp.dot(
        token_rows,
        lax.all_gather(w_kv, "col", axis=1, tiled=True),
        preferred_element_type=jnp.float32,
    ).astype(jnp.bfloat16)
    w_full = lax.all_gather(w_o, "col", axis=1, tiled=True)
    key_heads = keys_vals[:, :width_d].reshape(-1, HEADS, HEAD)
    val_heads = keys_vals[:, width_d:].reshape(-1, HEADS, HEAD)
    query_heads = queries.reshape(latent_count, HEADS, HEAD)
    score_scale = 1.0 / math.sqrt(HEAD)
    group_size = math.gcd(HEADS, 4)
    max_parts, den_parts, num_parts = ([], [], [])
    for first_head in range(0, HEADS, group_size):
        scores = (
            jnp.einsum(
                "lhd,thd->lht",
                query_heads[:, first_head : first_head + group_size],
                key_heads[:, first_head : first_head + group_size],
                preferred_element_type=jnp.float32,
            )
            * score_scale
        )
        local_max = jnp.max(scores, axis=-1)
        weights = jnp.exp(scores - local_max[..., None])
        den_parts.append(jnp.sum(weights, axis=-1))
        max_parts.append(local_max)
        num_parts.append(
            jnp.einsum(
                "lht,thd->lhd",
                weights.astype(jnp.bfloat16),
                val_heads[:, first_head : first_head + group_size],
                preferred_element_type=jnp.float32,
            )
        )
    maxima = jnp.concatenate(max_parts, axis=1)
    denom = jnp.concatenate(den_parts, axis=1)
    numer = jnp.concatenate(num_parts, axis=1)
    peak = lax.pmax(maxima, ("row", "col"))
    factor = jnp.exp(maxima - peak)
    den_terms = denom * factor
    num_terms = (numer * factor[..., None]).reshape(latent_count, width_d)
    den_part, num_part = (
        lax.psum_scatter(den_terms, "col", scatter_dimension=0, tiled=True),
        lax.psum_scatter(num_terms, "col", scatter_dimension=0, tiled=True),
    )
    den_share, num_share = lax.psum((den_part, num_part), "row")
    own_rows = finish_latents(
        num_share.reshape(num_share.shape[0], HEADS, HEAD), den_share, latent_gain, w_full
    )
    latents = lax.all_gather(own_rows, "col", axis=0, tiled=True)
    return (token_map, latents)


def solution(mesh):
    in_specs = (
        P("row", "col", None),
        P(),
        P(),
        P(),
        P(None, "col"),
        P("col", None),
        P(None, "col"),
        P(),
        P(),
        P(None, "col"),
    )
    out_specs = (P("row", "col", None), P())
    return jax.shard_map(kernel_body, mesh=mesh, in_specs=in_specs, out_specs=out_specs, check_vma=False)
```

```python
import functools
import math

import jax
import jax.numpy as jnp
from jax import lax
from jax.experimental import pallas as pl
from jax.experimental.pallas import tpu as pltpu
from jax.sharding import PartitionSpec as P

HEADS = 12
HEAD = 64
HALO = 3
EDGE = 8
LANES = 128
MESH = pl.DeviceIdType.MESH
VMEM_BYTES = 60 * 1024 * 1024


def log2(count):
    return count.bit_length() - 1


def barrier_with(peers):
    barrier = pltpu.get_barrier_semaphore()
    total = 0
    for cond, device in peers:
        if cond is None:
            pl.semaphore_signal(barrier, inc=1, device_id=device, device_id_type=MESH)
            total = total + 1
        else:

            @pl.when(cond)
            def _():
                pl.semaphore_signal(barrier, inc=1, device_id=device, device_id_type=MESH)

            total = total + jnp.where(cond, 1, 0)
    pl.semaphore_wait(barrier, total)


def block_kernel(
    rows,
    cols,
    tokens,
    dw,
    gain,
    shift,
    w_in,
    w_out,
    w_kv,
    w_o,
    queries,
    tok_out,
    num_out,
    stat_out,
    wo_out,
    g_in,
    g_out,
    g_kv,
    pad,
    mixed,
    normed,
    hidden,
    acc,
    tok_bf,
    kv,
    h_rows,
    h_cols,
    h_corners,
    halo_send,
    halo_recv,
    send_sem,
    recv_sem,
    local_sem,
):
    bits = log2(rows)
    row, col = lax.axis_index("row"), lax.axis_index("col")
    height, width, depth = tokens.shape
    count = height * width
    coords = [(row // (1 << (bits - 1 - i))) % 2 for i in range(bits)]

    def partner(dim):
        step = 1 << (bits - 1 - dim)
        return row + step * (1 - 2 * coords[dim])

    halo = []
    for dr in (-1, 0, 1):
        for dc in (-1, 0, 1):
            if dr == 0 and dc == 0:
                continue
            cond = None
            for d, pos, n in ((dr, row, rows), (dc, col, cols)):
                if d:
                    one = (pos + d >= 0) & (pos + d < n)
                    cond = one if cond is None else cond & one
            halo.append((dr, dc, cond))

    peers = [(cond, (row + dr, col + dc)) for dr, dc, cond in halo]
    peers += [(None, (row, (col + j) % cols)) for j in range(1, cols)]
    peers += [(None, (partner(i), col)) for i in range(bits)]
    barrier_with(peers)

    def halo_slot(dr, dc):
        if dc == 0:
            return h_rows.at[0 if dr < 0 else 1]
        if dr == 0:
            return h_cols.at[0 if dc < 0 else 1]
        return h_corners.at[(0 if dr < 0 else 2) + (0 if dc < 0 else 1)]

    def halo_copy(i, dr, dc):
        r_span = {-1: pl.ds(0, HALO), 0: slice(None), 1: pl.ds(height - HALO, HALO)}[dr]
        c_span = {-1: pl.ds(0, EDGE), 0: slice(None), 1: pl.ds(width - EDGE, EDGE)}[dc]
        src = tokens.at[r_span, c_span]
        return pltpu.make_async_remote_copy(
            src_ref=src,
            dst_ref=halo_slot(-dr, -dc),
            send_sem=halo_send.at[i],
            recv_sem=halo_recv.at[len(halo) - 1 - i],
            device_id=(row + dr, col + dc),
            device_id_type=MESH,
        )

    for i, (dr, dc, cond) in enumerate(halo):

        @pl.when(cond)
        def _():
            halo_copy(i, dr, dc).start()

    shards = (w_in, w_out, w_kv, w_o)
    fulls = (g_in, g_out, g_kv, wo_out)
    units = [(w, j) for w in range(4) for j in range(1, cols)]
    own = tuple(coords)

    halves = [len(w.shape) - bits - 2 for w in shards]
    ways = bits + (bits - 1) + 1

    def unit_copies(u, phase):
        w, j = units[u]
        slot = u * ways
        if phase == 0:
            target = (row, (col + cols - j) % cols)
            trips = [(shards[w].at[own], fulls[w].at[(col,) + own], target, slot)]
        else:
            block = (col + j) % cols
            split = halves[w] and phase < bits
            trips = []
            for half in range(2 if split else 1):
                order = list(range(bits - 1))
                if (half if split else u % 2):
                    order = order[::-1]
                order = order + [bits - 1]
                done = order[: phase - 1]
                idx = (block,) + tuple(slice(None) if i in done else own[i] for i in range(bits))
                if split:
                    idx = idx + (half,)
                ref = fulls[w].at[idx]
                at = slot + ways - 1 if phase == bits else slot + 1 + 2 * (phase - 1) + half
                trips.append((ref, ref, (partner(order[phase - 1]), col), at))
        return [
            pltpu.make_async_remote_copy(
                src_ref=src,
                dst_ref=dst,
                send_sem=send_sem.at[at],
                recv_sem=recv_sem.at[at],
                device_id=target,
                device_id_type=MESH,
            )
            for src, dst, target, at in trips
        ]

    for u in range(len(units)):
        for c in unit_copies(u, 0):
            c.start()
    local = []
    for w in range(4):
        copy = pltpu.make_async_copy(shards[w], fulls[w].at[col], local_sem.at[w])
        copy.start()
        local.append(copy)

    lag = 2
    state = {"tick": 0}
    ticks = len(units) + lag * bits

    def tick():
        t = state["tick"]
        if t >= ticks:
            return
        state["tick"] = t + 1
        for phase in range(bits, -1, -1):
            u = t - lag * phase
            if 0 <= u < len(units):
                for c in unit_copies(u, phase):
                    c.wait_recv()
                if phase < bits:
                    for c in unit_copies(u, phase + 1):
                        c.start()

    def finish_unit(u):
        while state["tick"] <= u + lag * bits:
            tick()

    pad[pl.ds(HALO, height), pl.ds(EDGE, width), :] = tokens[...].astype(jnp.float32)
    spans = {-1: (0, HALO), 0: (HALO, height), 1: (HALO + height, HALO)}
    lanes_of = {-1: (0, EDGE), 0: (EDGE, width), 1: (EDGE + width, EDGE)}
    for i, (dr, dc, cond) in enumerate(halo):
        r0, rn = spans[dr]
        c0, cn = lanes_of[dc]

        @pl.when(cond)
        def _():
            halo_copy(len(halo) - 1 - i, -dr, -dc).wait_recv()
            pad[pl.ds(r0, rn), pl.ds(c0, cn), :] = halo_slot(dr, dc)[...].astype(jnp.float32)

        @pl.when(jnp.logical_not(cond))
        def _():
            pad[pl.ds(r0, rn), pl.ds(c0, cn), :] = jnp.zeros((rn, cn, depth), jnp.float32)

    taps = 2 * HALO + 1
    chunks = depth // LANES

    def conv_rows(first, n_rows):
        def one(step, carry):
            i = first + step // chunks
            q = pl.multiple_of((step % chunks) * LANES, LANES)
            sums = [None] * taps
            for a in range(taps):
                line = pad[i + a, :, pl.ds(q, LANES)]
                for b in range(taps):
                    lo = 0 if b < HALO else EDGE
                    hi = EDGE + width + (EDGE if b > HALO else 0)
                    term = line[lo:hi] * dw[a, pl.ds(b, 1), pl.ds(q, LANES)]
                    sums[b] = term if sums[b] is None else sums[b] + term
            total = sums[HALO]
            for b in range(taps):
                if b == HALO:
                    continue
                size = width + EDGE
                offset = EDGE - HALO + b - (0 if b < HALO else EDGE)
                total = total + pltpu.roll(sums[b], (size - offset) % size, 0)[:width]
            mixed[i, :, pl.ds(q, LANES)] = total
            return carry

        lax.fori_loop(0, n_rows * chunks, one, 0)

    group = 2
    span = group * width

    def norm_rows(g, carry):
        value = mixed[pl.ds(g * group, group), :, :].reshape(span, depth)
        center = value - jnp.mean(value, axis=-1, keepdims=True)
        spread = jnp.mean(center * center, axis=-1, keepdims=True)
        out = center * lax.rsqrt(spread + 1e-06) * gain[...][None, :] + shift[...][None, :]
        normed[pl.ds(pl.multiple_of(g * span, 16), span), :] = out.astype(jnp.bfloat16)
        return carry

    quarter = height // 4
    for part in range(4):
        conv_rows(part * quarter, quarter)
        tick()
    lax.fori_loop(0, height // group, norm_rows, 0)
    for copy in local:
        copy.wait()

    def wide(ref, block, lo, size):
        value = ref[(block,) + (slice(None),) * (bits + 2) + (pl.ds(lo, size),)]
        return value.reshape(-1, size)

    f_width = w_in.shape[-1]
    tile = 256 if f_width % 256 == 0 else LANES

    def expand(block):
        def one(n, carry):
            lo = pl.multiple_of(n * tile, tile)
            u = jnp.dot(normed[...], wide(g_in, block, lo, tile), preferred_element_type=jnp.float32)
            hidden[block, :, pl.ds(lo, tile)] = jax.nn.gelu(u).astype(jnp.bfloat16)
            return carry

        lax.fori_loop(0, f_width // tile, one, 0)

    def contract(block, fresh):
        def one(n, carry):
            lo = pl.multiple_of(n * 256, 256)
            part = jnp.dot(
                hidden[block], wide(g_out, block, lo, 256), preferred_element_type=jnp.float32
            )
            if fresh:
                acc[:, pl.ds(lo, 256)] = part
            else:
                acc[:, pl.ds(lo, 256)] += part
            return carry

        lax.fori_loop(0, depth // 256, one, 0)

    expand(col)
    tick()
    contract(col, True)
    for j in range(1, cols):
        finish_unit(j - 1)
        expand((col + j) % cols)
    for j in range(1, cols):
        finish_unit(cols - 1 + j - 1)
        contract((col + j) % cols, False)

    def close_rows(g, carry):
        base = pad[pl.ds(HALO + g * group, group), pl.ds(EDGE, width), :].reshape(span, depth)
        at = pl.ds(pl.multiple_of(g * span, 16), span)
        total = base + acc[at, :]
        tok_out[pl.ds(g * group, group), :, :] = total.reshape(group, width, depth).astype(jnp.bfloat16)
        tok_bf[at, :] = total.astype(jnp.bfloat16)
        return carry

    lax.fori_loop(0, height // group, close_rows, 0)

    kv_width = w_kv.shape[-1]

    def project(block):
        def one(n, carry):
            lo = pl.multiple_of(n * LANES, LANES)
            out = jnp.dot(tok_bf[...], wide(g_kv, block, lo, LANES), preferred_element_type=jnp.float32)
            kv[block, :, pl.ds(lo, LANES)] = out.astype(jnp.bfloat16)
            return carry

        lax.fori_loop(0, kv_width // LANES, one, 0)

    project(col)
    for j in range(1, cols):
        finish_unit(2 * (cols - 1) + j - 1)
        project((col + j) % cols)

    latents = queries.shape[0]
    scale = 1.0 / math.sqrt(HEAD)
    stat_out[...] = jnp.zeros((latents, LANES), jnp.float32)
    side = lax.broadcasted_iota(jnp.int32, (1, LANES), 1)

    def attend(pair, carry):
        at = pl.multiple_of(pair * LANES, LANES)
        k_at, v_at = at, depth + at
        keys = kv[k_at // kv_width, :, pl.ds(pl.multiple_of(k_at % kv_width, LANES), LANES)]
        vals = kv[v_at // kv_width, :, pl.ds(pl.multiple_of(v_at % kv_width, LANES), LANES)]
        q = queries[:, pl.ds(at, LANES)]
        stat = stat_out[...]
        outs = []
        for s in range(2):
            keep = (side // HEAD) == s
            q_one = jnp.where(keep, q, jnp.zeros_like(q))
            scores = lax.dot_general(
                q_one, keys, (((1,), (1,)), ((), ())), preferred_element_type=jnp.float32
            )
            top = jnp.max(scores, axis=-1, keepdims=True)
            weights = jnp.exp((scores - top) * scale)
            den = jnp.sum(weights, axis=-1, keepdims=True)
            outs.append(
                jnp.dot(weights.astype(jnp.bfloat16), vals, preferred_element_type=jnp.float32)
            )
            lane = pair * 2 + s
            stat = jnp.where(side == lane, top * scale, stat)
            stat = jnp.where(side == lane + HEAD, den, stat)
        stat_out[...] = stat
        num_out[:, pl.ds(at, LANES)] = jnp.where(side < HEAD, outs[0], outs[1]).astype(jnp.bfloat16)
        return carry

    lax.fori_loop(0, depth // LANES, attend, 0)

    finish_unit(len(units) - 1)
    for i, (dr, dc, cond) in enumerate(halo):

        @pl.when(cond)
        def _():
            halo_copy(i, dr, dc).wait_send()

    for u in range(len(units)):
        for phase in range(bits + 1):
            for c in unit_copies(u, phase):
                c.wait_send()


def per_head(factors, n):
    side = lax.broadcasted_iota(jnp.int32, (1, LANES), 1)
    parts = []
    for pair in range(HEADS // 2):
        lo = jnp.broadcast_to(factors[:, 2 * pair : 2 * pair + 1], (n, LANES))
        hi = jnp.broadcast_to(factors[:, 2 * pair + 1 : 2 * pair + 2], (n, LANES))
        parts.append(jnp.where(side < HEAD, lo, hi))
    return jnp.concatenate(parts, axis=-1)


def merge(stats, nums):
    n = stats[0].shape[0]
    side = lax.broadcasted_iota(jnp.int32, (1, LANES), 1)
    peak = functools.reduce(jnp.maximum, stats)
    den, num = None, None
    for stat, part in zip(stats, nums):
        factor = jnp.exp(stat - peak)
        d = pltpu.roll(stat, HEAD, 1) * factor
        t = part.astype(jnp.float32) * per_head(factor, n)
        den = d if den is None else den + d
        num = t if num is None else num + t
    return jnp.where(side < HEAD, peak, pltpu.roll(den, HEAD, 1)), num


def latent_kernel(
    rows, cols, num_in, stat_in, latent_gain, out, num, stat, got_num, got_stat, send_sem, recv_sem
):
    bits = log2(rows)
    row, col = lax.axis_index("row"), lax.axis_index("col")
    latents = num_in.shape[0]

    def bit(i):
        return (row // (1 << i)) % 2

    def partner(i):
        return row + (1 << i) * (1 - 2 * bit(i))

    peers = [(None, (row, (col + j) % cols)) for j in range(1, cols)]
    peers += [(None, (partner(i), col)) for i in range(bits)]
    barrier_with(peers)

    def copy(src, dst, slot, device):
        return pltpu.make_async_remote_copy(
            src_ref=src,
            dst_ref=dst,
            send_sem=send_sem.at[slot],
            recv_sem=recv_sem.at[slot],
            device_id=device,
            device_id_type=MESH,
        )

    slot = 0
    sent = []
    base = 0
    size = latents
    offset = 0
    bases = []
    for i in range(bits):
        half = size // 2
        mine = base + bit(i) * half
        theirs = base + (1 - bit(i)) * half
        src_num, src_stat = (num_in, stat_in) if i == 0 else (num, stat)
        give = pl.ds(pl.multiple_of(theirs, 16), half)
        land = pl.ds(offset, half)
        pair = [
            copy(src_stat.at[give], got_stat.at[land], slot, (partner(i), col)),
            copy(src_num.at[give], got_num.at[land], slot + 1, (partner(i), col)),
        ]
        slot += 2
        for c in pair:
            c.start()
        for c in pair:
            c.wait_recv()
        sent += pair
        step = min(half, 32)

        def fold(k, carry):
            at = pl.ds(pl.multiple_of(mine + k * step, 16), step)
            came = pl.ds(pl.multiple_of(offset + k * step, 16), step)
            new_stat, new_num = merge(
                [src_stat[at, :], got_stat[came, :]], [src_num[at, :], got_num[came, :]]
            )
            stat[at, :] = new_stat
            num[at, :] = new_num.astype(jnp.bfloat16)
            return carry

        lax.fori_loop(0, half // step, fold, 0)
        bases.append((base, size))
        base, size, offset = mine, half, offset + half

    share = size // cols
    arrived = []
    for j in range(1, cols):
        other = (col + cols - j) % cols
        give = pl.ds(pl.multiple_of(base + other * share, 16), share)
        land = pl.ds(offset + (j - 1) * share, share)
        pair = [
            copy(stat.at[give], got_stat.at[land], slot, (row, other)),
            copy(num.at[give], got_num.at[land], slot + 1, (row, other)),
        ]
        slot += 2
        for c in pair:
            c.start()
        sent += pair
        arrived.append((pair, land))
    for pair, _ in arrived:
        for c in pair:
            c.wait_recv()
    own = pl.ds(pl.multiple_of(base + col * share, 16), share)
    final_stat, final_num = merge(
        [stat[own, :]] + [got_stat[land, :] for _, land in arrived],
        [num[own, :]] + [got_num[land, :] for _, land in arrived],
    )
    attended = final_num / per_head(pltpu.roll(final_stat, HEAD, 1), share)
    squares = jnp.mean(attended * attended, axis=-1, keepdims=True)
    scaled = attended * lax.rsqrt(squares + 1e-06) * latent_gain[...][None, :]
    out[own, :] = scaled.astype(jnp.bfloat16)

    gather = []
    for j in range(1, cols):
        c = copy(out.at[own], out.at[own], slot, (row, (col + cols - j) % cols))
        slot += 1
        c.start()
        gather.append(c)
    for c in gather:
        c.wait_recv()
    sent += gather
    for i in reversed(range(bits)):
        held = pl.ds(pl.multiple_of(base, 16), size)
        c = copy(out.at[held], out.at[held], slot, (partner(i), col))
        slot += 1
        c.start()
        c.wait_recv()
        sent.append(c)
        base, size = bases[i]
    for c in sent:
        c.wait_send()


def vmem(n):
    return [pl.BlockSpec(memory_space=pltpu.VMEM)] * n


def fits(mesh_rows, mesh_cols, tokens, w_in, w_kv, queries):
    height, width, depth = tokens.shape
    return (
        mesh_rows >= 2
        and mesh_cols >= 2
        and mesh_rows & (mesh_rows - 1) == 0
        and depth % (32 * mesh_rows) == 0
        and w_in.shape[1] % LANES == 0
        and w_in.shape[1] % (32 * mesh_rows) == 0
        and depth // mesh_cols % (8 * mesh_rows) == 0
        and w_kv.shape[1] % LANES == 0
        and queries.shape[0] % (16 * mesh_rows * mesh_cols) == 0
        and depth % 256 == 0
        and height % 4 == 0
        and width % 8 == 0
        and 2 * width % 16 == 0
    )


def kernel_body(tokens, dw_kernel, norm_gain, norm_shift, w_in, w_out, w_kv, queries, latent_gain, w_o):
    rows, cols = lax.axis_size("row"), lax.axis_size("col")
    height, width, depth = tokens.shape
    if not fits(rows, cols, tokens, w_in, w_kv, queries):
        return body(
            tokens, dw_kernel, norm_gain, norm_shift, w_in, w_out, w_kv, queries, latent_gain, w_o
        )
    bits = log2(rows)
    count = height * width
    latents = queries.shape[0]
    f_width = w_in.shape[1]
    grid = (2,) * bits
    bf16, f32 = jnp.bfloat16, jnp.float32

    def cut(w, parts):
        tail = (2, w.shape[0] // rows // 2) if parts == 2 else (w.shape[0] // rows,)
        return w.reshape(grid + tail + (w.shape[1],))

    shards = [cut(w_in, 2), cut(w_out, 2), cut(w_kv, 2), cut(w_o.T, 1)]
    units = 4 * (cols - 1)
    token_map, num, stat, wo_full = pl.pallas_call(
        functools.partial(block_kernel, rows, cols),
        out_shape=(
            jax.ShapeDtypeStruct(tokens.shape, bf16),
            jax.ShapeDtypeStruct((latents, depth), bf16),
            jax.ShapeDtypeStruct((latents, LANES), f32),
            jax.ShapeDtypeStruct((cols,) + shards[3].shape, bf16),
        ),
        in_specs=vmem(9),
        out_specs=tuple(vmem(4)),
        scratch_shapes=[
            pltpu.VMEM((cols,) + shards[0].shape, bf16),
            pltpu.VMEM((cols,) + shards[1].shape, bf16),
            pltpu.VMEM((cols,) + shards[2].shape, bf16),
            pltpu.VMEM((height + 2 * HALO, width + 2 * EDGE, depth), f32),
            pltpu.VMEM((height, width, depth), f32),
            pltpu.VMEM((count, depth), bf16),
            pltpu.VMEM((cols, count, f_width), bf16),
            pltpu.VMEM((count, depth), f32),
            pltpu.VMEM((count, depth), bf16),
            pltpu.VMEM((cols, count, w_kv.shape[1]), bf16),
            pltpu.VMEM((2, HALO, width, depth), bf16),
            pltpu.VMEM((2, height, EDGE, depth), bf16),
            pltpu.VMEM((4, HALO, EDGE, depth), bf16),
            pltpu.SemaphoreType.DMA((8,)),
            pltpu.SemaphoreType.DMA((8,)),
            pltpu.SemaphoreType.DMA((units * 2 * bits,)),
            pltpu.SemaphoreType.DMA((units * 2 * bits,)),
            pltpu.SemaphoreType.DMA((4,)),
        ],
        compiler_params=pltpu.CompilerParams(
            collective_id=0, has_side_effects=True, vmem_limit_bytes=VMEM_BYTES
        ),
        name="block",
    )(
        tokens,
        dw_kernel,
        norm_gain,
        norm_shift,
        *shards,
        queries,
    )
    slots = 2 * bits + 3 * (cols - 1) + bits
    scaled = pl.pallas_call(
        functools.partial(latent_kernel, rows, cols),
        out_shape=jax.ShapeDtypeStruct((latents, depth), bf16),
        in_specs=vmem(3),
        out_specs=vmem(1)[0],
        scratch_shapes=[
            pltpu.VMEM((latents, depth), bf16),
            pltpu.VMEM((latents, LANES), f32),
            pltpu.VMEM((latents, depth), bf16),
            pltpu.VMEM((latents, LANES), f32),
            pltpu.SemaphoreType.DMA((slots,)),
            pltpu.SemaphoreType.DMA((slots,)),
        ],
        compiler_params=pltpu.CompilerParams(
            collective_id=1, has_side_effects=True, vmem_limit_bytes=VMEM_BYTES
        ),
        name="latents",
    )(num, stat, latent_gain)
    w_turned = wo_full.reshape(-1, depth)
    latents_out = lax.dot_general(
        scaled, w_turned, (((1,), (1,)), ((), ())), preferred_element_type=f32
    ).astype(bf16)
    return (token_map, latents_out)


def with_halo(cells, sides, width):
    for axis, dim in sides:
        count = lax.axis_size(axis)
        ends = count - 1
        head = lax.slice_in_dim(cells, 0, width, axis=dim)
        tail = lax.slice_in_dim(cells, cells.shape[dim] - width, cells.shape[dim], axis=dim)
        cells = jnp.concatenate(
            [
                lax.ppermute(tail, axis, [(i, (i + 1) % count) for i in range(ends)]),
                cells,
                lax.ppermute(head, axis, [((i + 1) % count, i) for i in range(ends)]),
            ],
            axis=dim,
        )
    return cells


def conv_taps(padded, height, width, dw_kernel):
    mixed = jnp.zeros((height, width, padded.shape[2]), jnp.float32)
    for row_tap in range(7):
        for col_tap in range(7):
            mixed = (
                mixed
                + padded[row_tap : row_tap + height, col_tap : col_tap + width]
                * dw_kernel[row_tap, col_tap]
            )
    return mixed


def layer_norm(mixed, norm_gain, norm_shift):
    center = mixed - jnp.mean(mixed, axis=-1, keepdims=True)
    spread = jnp.mean(center * center, axis=-1, keepdims=True)
    return (center * lax.rsqrt(spread + 1e-06) * norm_gain + norm_shift).astype(jnp.bfloat16)


def finish_latents(numer, denom, latent_gain, w_full):
    attended = (numer / denom[..., None]).reshape(numer.shape[0], -1)
    squares = jnp.mean(attended * attended, axis=-1, keepdims=True)
    scaled = (attended * lax.rsqrt(squares + 1e-06) * latent_gain).astype(jnp.bfloat16)
    return jnp.dot(scaled, w_full, preferred_element_type=jnp.float32).astype(jnp.bfloat16)


def body(tokens, dw_kernel, norm_gain, norm_shift, w_in, w_out, w_kv, queries, latent_gain, w_o):
    height, width, width_d = tokens.shape
    latent_count = queries.shape[0]
    padded = with_halo(tokens, (("row", 0), ("col", 1)), 3)
    mixed = conv_taps(padded.astype(jnp.float32), height, width, dw_kernel)
    normed = layer_norm(mixed, norm_gain, norm_shift).reshape(height * width, width_d)
    residual = tokens.reshape(height * width, width_d).astype(jnp.float32)
    hidden = jax.nn.gelu(
        jnp.dot(
            normed,
            lax.all_gather(w_in, "col", axis=1, tiled=True),
            preferred_element_type=jnp.float32,
        )
    ).astype(jnp.bfloat16)
    update = jnp.dot(
        hidden, lax.all_gather(w_out, "col", axis=0, tiled=True), preferred_element_type=jnp.float32
    )
    token_rows = (residual + update).astype(jnp.bfloat16)
    token_map = token_rows.reshape(height, width, width_d)
    keys_vals = jnp.dot(
        token_rows,
        lax.all_gather(w_kv, "col", axis=1, tiled=True),
        preferred_element_type=jnp.float32,
    ).astype(jnp.bfloat16)
    w_full = lax.all_gather(w_o, "col", axis=1, tiled=True)
    key_heads = keys_vals[:, :width_d].reshape(-1, HEADS, HEAD)
    val_heads = keys_vals[:, width_d:].reshape(-1, HEADS, HEAD)
    query_heads = queries.reshape(latent_count, HEADS, HEAD)
    score_scale = 1.0 / math.sqrt(HEAD)
    group_size = math.gcd(HEADS, 4)
    max_parts, den_parts, num_parts = ([], [], [])
    for first_head in range(0, HEADS, group_size):
        scores = (
            jnp.einsum(
                "lhd,thd->lht",
                query_heads[:, first_head : first_head + group_size],
                key_heads[:, first_head : first_head + group_size],
                preferred_element_type=jnp.float32,
            )
            * score_scale
        )
        local_max = jnp.max(scores, axis=-1)
        weights = jnp.exp(scores - local_max[..., None])
        den_parts.append(jnp.sum(weights, axis=-1))
        max_parts.append(local_max)
        num_parts.append(
            jnp.einsum(
                "lht,thd->lhd",
                weights.astype(jnp.bfloat16),
                val_heads[:, first_head : first_head + group_size],
                preferred_element_type=jnp.float32,
            )
        )
    maxima = jnp.concatenate(max_parts, axis=1)
    denom = jnp.concatenate(den_parts, axis=1)
    numer = jnp.concatenate(num_parts, axis=1)
    peak = lax.pmax(maxima, ("row", "col"))
    factor = jnp.exp(maxima - peak)
    den_terms = denom * factor
    num_terms = (numer * factor[..., None]).reshape(latent_count, width_d)
    den_part, num_part = (
        lax.psum_scatter(den_terms, "col", scatter_dimension=0, tiled=True),
        lax.psum_scatter(num_terms, "col", scatter_dimension=0, tiled=True),
    )
    den_share, num_share = lax.psum((den_part, num_part), "row")
    own_rows = finish_latents(
        num_share.reshape(num_share.shape[0], HEADS, HEAD), den_share, latent_gain, w_full
    )
    latents = lax.all_gather(own_rows, "col", axis=0, tiled=True)
    return (token_map, latents)


def solution(mesh):
    in_specs = (
        P("row", "col", None),
        P(),
        P(),
        P(),
        P(None, "col"),
        P("col", None),
        P(None, "col"),
        P(),
        P(),
        P(None, "col"),
    )
    out_specs = (P("row", "col", None), P())
    return jax.shard_map(kernel_body, mesh=mesh, in_specs=in_specs, out_specs=out_specs, check_vma=False)
```

```python
import functools
import math

import jax
import jax.numpy as jnp
from jax import lax
from jax.experimental import pallas as pl
from jax.experimental.pallas import tpu as pltpu
from jax.sharding import PartitionSpec as P

HEADS = 12
HEAD = 64
HALO = 3
EDGE = 8
LANES = 128
MESH = pl.DeviceIdType.MESH
VMEM_BYTES = 60 * 1024 * 1024


def log2(count):
    return count.bit_length() - 1


def barrier_with(peers):
    barrier = pltpu.get_barrier_semaphore()
    total = 0
    for cond, device in peers:
        if cond is None:
            pl.semaphore_signal(barrier, inc=1, device_id=device, device_id_type=MESH)
            total = total + 1
        else:

            @pl.when(cond)
            def _():
                pl.semaphore_signal(barrier, inc=1, device_id=device, device_id_type=MESH)

            total = total + jnp.where(cond, 1, 0)
    pl.semaphore_wait(barrier, total)


def block_kernel(
    rows,
    cols,
    tokens,
    dw,
    gain,
    shift,
    w_in,
    w_out,
    w_kv,
    w_o,
    queries,
    tok_out,
    num_out,
    stat_out,
    wo_out,
    g_in,
    g_out,
    g_kv,
    pad,
    mixed,
    normed,
    hidden,
    acc,
    tok_bf,
    kv,
    h_rows,
    h_cols,
    h_corners,
    halo_send,
    halo_recv,
    send_sem,
    recv_sem,
    local_sem,
):
    bits = log2(rows)
    row, col = lax.axis_index("row"), lax.axis_index("col")
    height, width, depth = tokens.shape
    count = height * width
    coords = [(row // (1 << (bits - 1 - i))) % 2 for i in range(bits)]

    def partner(dim):
        step = 1 << (bits - 1 - dim)
        return row + step * (1 - 2 * coords[dim])

    halo = []
    for dr in (-1, 0, 1):
        for dc in (-1, 0, 1):
            if dr == 0 and dc == 0:
                continue
            cond = None
            for d, pos, n in ((dr, row, rows), (dc, col, cols)):
                if d:
                    one = (pos + d >= 0) & (pos + d < n)
                    cond = one if cond is None else cond & one
            halo.append((dr, dc, cond))

    peers = [(cond, (row + dr, col + dc)) for dr, dc, cond in halo]
    peers += [(None, (row, (col + j) % cols)) for j in range(1, cols)]
    peers += [(None, (partner(i), col)) for i in range(bits)]
    barrier_with(peers)

    def halo_slot(dr, dc):
        if dc == 0:
            return h_rows.at[0 if dr < 0 else 1]
        if dr == 0:
            return h_cols.at[0 if dc < 0 else 1]
        return h_corners.at[(0 if dr < 0 else 2) + (0 if dc < 0 else 1)]

    def halo_copy(i, dr, dc):
        r_span = {-1: pl.ds(0, HALO), 0: slice(None), 1: pl.ds(height - HALO, HALO)}[dr]
        c_span = {-1: pl.ds(0, EDGE), 0: slice(None), 1: pl.ds(width - EDGE, EDGE)}[dc]
        src = tokens.at[r_span, c_span]
        return pltpu.make_async_remote_copy(
            src_ref=src,
            dst_ref=halo_slot(-dr, -dc),
            send_sem=halo_send.at[i],
            recv_sem=halo_recv.at[len(halo) - 1 - i],
            device_id=(row + dr, col + dc),
            device_id_type=MESH,
        )

    for i, (dr, dc, cond) in enumerate(halo):

        @pl.when(cond)
        def _():
            halo_copy(i, dr, dc).start()

    shards = (w_in, w_out, w_kv, w_o)
    fulls = (g_in, g_out, g_kv, wo_out)
    units = [(w, j) for w in range(4) for j in range(1, cols)]
    own = tuple(coords)

    halves = [len(w.shape) - bits - 2 for w in shards]
    ways = bits + (bits - 1) + 1

    def unit_copies(u, phase):
        w, j = units[u]
        slot = u * ways
        if phase == 0:
            target = (row, (col + cols - j) % cols)
            trips = [(shards[w].at[own], fulls[w].at[(col,) + own], target, slot)]
        else:
            block = (col + j) % cols
            split = halves[w] and phase < bits
            trips = []
            for half in range(2 if split else 1):
                order = list(range(bits - 1))
                if (half if split else u % 2):
                    order = order[::-1]
                order = order + [bits - 1]
                done = order[: phase - 1]
                idx = (block,) + tuple(slice(None) if i in done else own[i] for i in range(bits))
                if split:
                    idx = idx + (half,)
                ref = fulls[w].at[idx]
                at = slot + ways - 1 if phase == bits else slot + 1 + 2 * (phase - 1) + half
                trips.append((ref, ref, (partner(order[phase - 1]), col), at))
        return [
            pltpu.make_async_remote_copy(
                src_ref=src,
                dst_ref=dst,
                send_sem=send_sem.at[at],
                recv_sem=recv_sem.at[at],
                device_id=target,
                device_id_type=MESH,
            )
            for src, dst, target, at in trips
        ]

    for u in range(len(units)):
        for c in unit_copies(u, 0):
            c.start()
    local = []
    for w in range(4):
        copy = pltpu.make_async_copy(shards[w], fulls[w].at[col], local_sem.at[w])
        copy.start()
        local.append(copy)

    lag = 2
    state = {"tick": 0}
    ticks = len(units) + lag * bits

    def tick():
        t = state["tick"]
        if t >= ticks:
            return
        state["tick"] = t + 1
        for phase in range(bits, -1, -1):
            u = t - lag * phase
            if 0 <= u < len(units):
                for c in unit_copies(u, phase):
                    c.wait_recv()
                if phase < bits:
                    for c in unit_copies(u, phase + 1):
                        c.start()

    def finish_unit(u):
        while state["tick"] <= u + lag * bits:
            tick()

    pad[pl.ds(HALO, height), pl.ds(EDGE, width), :] = tokens[...].astype(jnp.float32)
    spans = {-1: (0, HALO), 0: (HALO, height), 1: (HALO + height, HALO)}
    lanes_of = {-1: (0, EDGE), 0: (EDGE, width), 1: (EDGE + width, EDGE)}
    for i, (dr, dc, cond) in enumerate(halo):
        r0, rn = spans[dr]
        c0, cn = lanes_of[dc]

        @pl.when(cond)
        def _():
            halo_copy(len(halo) - 1 - i, -dr, -dc).wait_recv()
            pad[pl.ds(r0, rn), pl.ds(c0, cn), :] = halo_slot(dr, dc)[...].astype(jnp.float32)

        @pl.when(jnp.logical_not(cond))
        def _():
            pad[pl.ds(r0, rn), pl.ds(c0, cn), :] = jnp.zeros((rn, cn, depth), jnp.float32)

    taps = 2 * HALO + 1
    chunks = depth // LANES

    def conv_rows(first, n_rows):
        def one(step, carry):
            i = first + step // chunks
            q = pl.multiple_of((step % chunks) * LANES, LANES)
            sums = [None] * taps
            for a in range(taps):
                line = pad[i + a, :, pl.ds(q, LANES)]
                for b in range(taps):
                    lo = 0 if b < HALO else EDGE
                    hi = EDGE + width + (EDGE if b > HALO else 0)
                    term = line[lo:hi] * dw[a, pl.ds(b, 1), pl.ds(q, LANES)]
                    sums[b] = term if sums[b] is None else sums[b] + term
            total = sums[HALO]
            for b in range(taps):
                if b == HALO:
                    continue
                size = width + EDGE
                offset = EDGE - HALO + b - (0 if b < HALO else EDGE)
                total = total + pltpu.roll(sums[b], (size - offset) % size, 0)[:width]
            mixed[i, :, pl.ds(q, LANES)] = total
            return carry

        lax.fori_loop(0, n_rows * chunks, one, 0)

    group = 2
    span = group * width

    def norm_rows(g, carry):
        value = mixed[pl.ds(g * group, group), :, :].reshape(span, depth)
        center = value - jnp.mean(value, axis=-1, keepdims=True)
        spread = jnp.mean(center * center, axis=-1, keepdims=True)
        out = center * lax.rsqrt(spread + 1e-06) * gain[...][None, :] + shift[...][None, :]
        normed[pl.ds(pl.multiple_of(g * span, 16), span), :] = out.astype(jnp.bfloat16)
        return carry

    quarter = height // 4
    for part in range(4):
        conv_rows(part * quarter, quarter)
        tick()
    lax.fori_loop(0, height // group, norm_rows, 0)
    for copy in local:
        copy.wait()

    def wide(ref, block, lo, size):
        value = ref[(block,) + (slice(None),) * (bits + 2) + (pl.ds(lo, size),)]
        return value.reshape(-1, size)

    f_width = w_in.shape[-1]
    tile = 256 if f_width % 256 == 0 else LANES

    def expand(block):
        def one(n, carry):
            lo = pl.multiple_of(n * tile, tile)
            u = jnp.dot(normed[...], wide(g_in, block, lo, tile), preferred_element_type=jnp.float32)
            hidden[block, :, pl.ds(lo, tile)] = jax.nn.gelu(u).astype(jnp.bfloat16)
            return carry

        lax.fori_loop(0, f_width // tile, one, 0)

    def contract(block, fresh):
        def one(n, carry):
            lo = pl.multiple_of(n * 256, 256)
            part = jnp.dot(
                hidden[block], wide(g_out, block, lo, 256), preferred_element_type=jnp.float32
            )
            if fresh:
                acc[:, pl.ds(lo, 256)] = part
            else:
                acc[:, pl.ds(lo, 256)] += part
            return carry

        lax.fori_loop(0, depth // 256, one, 0)

    expand(col)
    tick()
    contract(col, True)
    for j in range(1, cols):
        finish_unit(j - 1)
        expand((col + j) % cols)
    for j in range(1, cols):
        finish_unit(cols - 1 + j - 1)
        contract((col + j) % cols, False)

    def close_rows(g, carry):
        base = pad[pl.ds(HALO + g * group, group), pl.ds(EDGE, width), :].reshape(span, depth)
        at = pl.ds(pl.multiple_of(g * span, 16), span)
        total = base + acc[at, :]
        tok_out[pl.ds(g * group, group), :, :] = total.reshape(group, width, depth).astype(jnp.bfloat16)
        tok_bf[at, :] = total.astype(jnp.bfloat16)
        return carry

    lax.fori_loop(0, height // group, close_rows, 0)

    kv_width = w_kv.shape[-1]

    def project(block):
        def one(n, carry):
            lo = pl.multiple_of(n * LANES, LANES)
            out = jnp.dot(tok_bf[...], wide(g_kv, block, lo, LANES), preferred_element_type=jnp.float32)
            kv[block, :, pl.ds(lo, LANES)] = out.astype(jnp.bfloat16)
            return carry

        lax.fori_loop(0, kv_width // LANES, one, 0)

    project(col)
    for j in range(1, cols):
        finish_unit(2 * (cols - 1) + j - 1)
        project((col + j) % cols)

    latents = queries.shape[0]
    scale = 1.0 / math.sqrt(HEAD)
    stat_out[...] = jnp.zeros((latents, LANES), jnp.float32)
    side = lax.broadcasted_iota(jnp.int32, (1, LANES), 1)

    def attend(pair, carry):
        at = pl.multiple_of(pair * LANES, LANES)
        k_at, v_at = at, depth + at
        keys = kv[k_at // kv_width, :, pl.ds(pl.multiple_of(k_at % kv_width, LANES), LANES)]
        vals = kv[v_at // kv_width, :, pl.ds(pl.multiple_of(v_at % kv_width, LANES), LANES)]
        q = queries[:, pl.ds(at, LANES)]
        stat = stat_out[...]
        outs = []
        for s in range(2):
            keep = (side // HEAD) == s
            q_one = jnp.where(keep, q, jnp.zeros_like(q))
            scores = lax.dot_general(
                q_one, keys, (((1,), (1,)), ((), ())), preferred_element_type=jnp.float32
            )
            top = jnp.max(scores, axis=-1, keepdims=True)
            weights = jnp.exp((scores - top) * scale)
            den = jnp.sum(weights, axis=-1, keepdims=True)
            outs.append(
                jnp.dot(weights.astype(jnp.bfloat16), vals, preferred_element_type=jnp.float32)
            )
            lane = pair * 2 + s
            stat = jnp.where(side == lane, top * scale, stat)
            stat = jnp.where(side == lane + HEAD, den, stat)
        stat_out[...] = stat
        num_out[:, pl.ds(at, LANES)] = jnp.where(side < HEAD, outs[0], outs[1]).astype(jnp.bfloat16)
        return carry

    lax.fori_loop(0, depth // LANES, attend, 0)

    finish_unit(len(units) - 1)
    for i, (dr, dc, cond) in enumerate(halo):

        @pl.when(cond)
        def _():
            halo_copy(i, dr, dc).wait_send()

    for u in range(len(units)):
        for phase in range(bits + 1):
            for c in unit_copies(u, phase):
                c.wait_send()


def per_head(factors, n):
    side = lax.broadcasted_iota(jnp.int32, (1, LANES), 1)
    parts = []
    for pair in range(HEADS // 2):
        lo = jnp.broadcast_to(factors[:, 2 * pair : 2 * pair + 1], (n, LANES))
        hi = jnp.broadcast_to(factors[:, 2 * pair + 1 : 2 * pair + 2], (n, LANES))
        parts.append(jnp.where(side < HEAD, lo, hi))
    return jnp.concatenate(parts, axis=-1)


def merge(stats, nums):
    n = stats[0].shape[0]
    side = lax.broadcasted_iota(jnp.int32, (1, LANES), 1)
    peak = functools.reduce(jnp.maximum, stats)
    den, num = None, None
    for stat, part in zip(stats, nums):
        factor = jnp.exp(stat - peak)
        d = pltpu.roll(stat, HEAD, 1) * factor
        t = part.astype(jnp.float32) * per_head(factor, n)
        den = d if den is None else den + d
        num = t if num is None else num + t
    return jnp.where(side < HEAD, peak, pltpu.roll(den, HEAD, 1)), num


def latent_kernel(
    rows, cols, num_in, stat_in, latent_gain, out, num, stat, got_num, got_stat, send_sem, recv_sem
):
    bits = log2(rows)
    row, col = lax.axis_index("row"), lax.axis_index("col")
    latents = num_in.shape[0]

    def bit(i):
        return (row // (1 << i)) % 2

    def partner(i):
        return row + (1 << i) * (1 - 2 * bit(i))

    peers = [(None, (row, (col + j) % cols)) for j in range(1, cols)]
    peers += [(None, (partner(i), col)) for i in range(bits)]
    barrier_with(peers)

    def copy(src, dst, slot, device):
        return pltpu.make_async_remote_copy(
            src_ref=src,
            dst_ref=dst,
            send_sem=send_sem.at[slot],
            recv_sem=recv_sem.at[slot],
            device_id=device,
            device_id_type=MESH,
        )

    sent = []
    slots = iter(range(4 * bits + 3 * (cols - 1) + 2 * bits))
    rest = list(range(1, bits))
    orders = [[0] + rest, [0] + rest[::-1]]
    held = [[], []]
    offset = 0
    trips = {}

    def exchange(s, p):
        nonlocal offset
        i = orders[s][p]
        if p == 0:
            size = latents // 4
            mine = bit(i) * 2 * size + s * size
            theirs = (1 - bit(i)) * 2 * size + s * size
        else:
            base, whole = held[s][-1]
            size = whole // 2
            mine, theirs = base + bit(i) * size, base + (1 - bit(i)) * size
        src_num, src_stat = (num_in, stat_in) if p == 0 else (num, stat)
        give = pl.ds(pl.multiple_of(theirs, 16), size)
        land = pl.ds(offset, size)
        pair = [
            copy(src_stat.at[give], got_stat.at[land], next(slots), (partner(i), col)),
            copy(src_num.at[give], got_num.at[land], next(slots), (partner(i), col)),
        ]
        for c in pair:
            c.start()
        trips[s, p] = (pair, offset)
        held[s].append((mine, size))
        offset = offset + size

    def collect(s, p):
        pair, first = trips[s, p]
        for c in pair:
            c.wait_recv()
        sent.extend(pair)
        mine, size = held[s][p]
        src_num, src_stat = (num_in, stat_in) if p == 0 else (num, stat)
        step = min(size, 32)

        def fold(k, carry):
            at = pl.ds(pl.multiple_of(mine + k * step, 16), step)
            came = pl.ds(pl.multiple_of(first + k * step, 16), step)
            new_stat, new_num = merge(
                [src_stat[at, :], got_stat[came, :]], [src_num[at, :], got_num[came, :]]
            )
            stat[at, :] = new_stat
            num[at, :] = new_num.astype(jnp.bfloat16)
            return carry

        lax.fori_loop(0, size // step, fold, 0)

    for s in range(2):
        exchange(s, 0)
    for p in range(bits):
        for s in range(2):
            collect(s, p)
            if p + 1 < bits:
                exchange(s, p + 1)

    share = latents // (rows * cols)
    side_cols = cols // 2

    def chunk(c):
        base = jnp.where(
            c < side_cols, held[0][-1][0] + c * share, held[1][-1][0] + (c - side_cols) * share
        )
        return pl.ds(pl.multiple_of(base, 16), share)

    arrived = []
    for j in range(1, cols):
        other = (col + cols - j) % cols
        land = pl.ds(offset + (j - 1) * share, share)
        pair = [
            copy(stat.at[chunk(other)], got_stat.at[land], next(slots), (row, other)),
            copy(num.at[chunk(other)], got_num.at[land], next(slots), (row, other)),
        ]
        for c in pair:
            c.start()
        sent += pair
        arrived.append((pair, land))
    for pair, _ in arrived:
        for c in pair:
            c.wait_recv()
    own = chunk(col)
    final_stat, final_num = merge(
        [stat[own, :]] + [got_stat[land, :] for _, land in arrived],
        [num[own, :]] + [got_num[land, :] for _, land in arrived],
    )
    attended = final_num / per_head(pltpu.roll(final_stat, HEAD, 1), share)
    squares = jnp.mean(attended * attended, axis=-1, keepdims=True)
    scaled = attended * lax.rsqrt(squares + 1e-06) * latent_gain[...][None, :]
    out[own, :] = scaled.astype(jnp.bfloat16)

    gather = []
    for j in range(1, cols):
        c = copy(out.at[own], out.at[own], next(slots), (row, (col + cols - j) % cols))
        c.start()
        gather.append(c)
    for c in gather:
        c.wait_recv()
    sent += gather
    back = [None, None]
    for p in reversed(range(bits)):
        for s in range(2):
            if back[s] is not None:
                back[s].wait_recv()
            base, size = held[s][p]
            rows_held = pl.ds(pl.multiple_of(base, 16), size)
            back[s] = copy(
                out.at[rows_held], out.at[rows_held], next(slots), (partner(orders[s][p]), col)
            )
            back[s].start()
            sent.append(back[s])
    for s in range(2):
        back[s].wait_recv()
    for c in sent:
        c.wait_send()


def vmem(n):
    return [pl.BlockSpec(memory_space=pltpu.VMEM)] * n


def fits(mesh_rows, mesh_cols, tokens, w_in, w_kv, queries):
    height, width, depth = tokens.shape
    return (
        mesh_rows >= 2
        and mesh_cols >= 2
        and mesh_cols % 2 == 0
        and mesh_rows & (mesh_rows - 1) == 0
        and depth % (32 * mesh_rows) == 0
        and w_in.shape[1] % LANES == 0
        and w_in.shape[1] % (32 * mesh_rows) == 0
        and depth // mesh_cols % (8 * mesh_rows) == 0
        and w_kv.shape[1] % LANES == 0
        and queries.shape[0] % (16 * mesh_rows * mesh_cols) == 0
        and depth % 256 == 0
        and height % 4 == 0
        and width % 8 == 0
        and 2 * width % 16 == 0
    )


def kernel_body(tokens, dw_kernel, norm_gain, norm_shift, w_in, w_out, w_kv, queries, latent_gain, w_o):
    rows, cols = lax.axis_size("row"), lax.axis_size("col")
    height, width, depth = tokens.shape
    if not fits(rows, cols, tokens, w_in, w_kv, queries):
        return body(
            tokens, dw_kernel, norm_gain, norm_shift, w_in, w_out, w_kv, queries, latent_gain, w_o
        )
    bits = log2(rows)
    count = height * width
    latents = queries.shape[0]
    f_width = w_in.shape[1]
    grid = (2,) * bits
    bf16, f32 = jnp.bfloat16, jnp.float32

    def cut(w, parts):
        tail = (2, w.shape[0] // rows // 2) if parts == 2 else (w.shape[0] // rows,)
        return w.reshape(grid + tail + (w.shape[1],))

    shards = [cut(w_in, 2), cut(w_out, 2), cut(w_kv, 2), cut(w_o.T, 1)]
    units = 4 * (cols - 1)
    token_map, num, stat, wo_full = pl.pallas_call(
        functools.partial(block_kernel, rows, cols),
        out_shape=(
            jax.ShapeDtypeStruct(tokens.shape, bf16),
            jax.ShapeDtypeStruct((latents, depth), bf16),
            jax.ShapeDtypeStruct((latents, LANES), f32),
            jax.ShapeDtypeStruct((cols,) + shards[3].shape, bf16),
        ),
        in_specs=vmem(9),
        out_specs=tuple(vmem(4)),
        scratch_shapes=[
            pltpu.VMEM((cols,) + shards[0].shape, bf16),
            pltpu.VMEM((cols,) + shards[1].shape, bf16),
            pltpu.VMEM((cols,) + shards[2].shape, bf16),
            pltpu.VMEM((height + 2 * HALO, width + 2 * EDGE, depth), f32),
            pltpu.VMEM((height, width, depth), f32),
            pltpu.VMEM((count, depth), bf16),
            pltpu.VMEM((cols, count, f_width), bf16),
            pltpu.VMEM((count, depth), f32),
            pltpu.VMEM((count, depth), bf16),
            pltpu.VMEM((cols, count, w_kv.shape[1]), bf16),
            pltpu.VMEM((2, HALO, width, depth), bf16),
            pltpu.VMEM((2, height, EDGE, depth), bf16),
            pltpu.VMEM((4, HALO, EDGE, depth), bf16),
            pltpu.SemaphoreType.DMA((8,)),
            pltpu.SemaphoreType.DMA((8,)),
            pltpu.SemaphoreType.DMA((units * 2 * bits,)),
            pltpu.SemaphoreType.DMA((units * 2 * bits,)),
            pltpu.SemaphoreType.DMA((4,)),
        ],
        compiler_params=pltpu.CompilerParams(
            collective_id=0, has_side_effects=True, vmem_limit_bytes=VMEM_BYTES
        ),
        name="block",
    )(
        tokens,
        dw_kernel,
        norm_gain,
        norm_shift,
        *shards,
        queries,
    )
    slots = 4 * bits + 3 * (cols - 1) + 2 * bits
    scaled = pl.pallas_call(
        functools.partial(latent_kernel, rows, cols),
        out_shape=jax.ShapeDtypeStruct((latents, depth), bf16),
        in_specs=vmem(3),
        out_specs=vmem(1)[0],
        scratch_shapes=[
            pltpu.VMEM((latents, depth), bf16),
            pltpu.VMEM((latents, LANES), f32),
            pltpu.VMEM((latents, depth), bf16),
            pltpu.VMEM((latents, LANES), f32),
            pltpu.SemaphoreType.DMA((slots,)),
            pltpu.SemaphoreType.DMA((slots,)),
        ],
        compiler_params=pltpu.CompilerParams(
            collective_id=1, has_side_effects=True, vmem_limit_bytes=VMEM_BYTES
        ),
        name="latents",
    )(num, stat, latent_gain)
    w_turned = wo_full.reshape(-1, depth)
    latents_out = lax.dot_general(
        scaled, w_turned, (((1,), (1,)), ((), ())), preferred_element_type=f32
    ).astype(bf16)
    return (token_map, latents_out)


def with_halo(cells, sides, width):
    for axis, dim in sides:
        count = lax.axis_size(axis)
        ends = count - 1
        head = lax.slice_in_dim(cells, 0, width, axis=dim)
        tail = lax.slice_in_dim(cells, cells.shape[dim] - width, cells.shape[dim], axis=dim)
        cells = jnp.concatenate(
            [
                lax.ppermute(tail, axis, [(i, (i + 1) % count) for i in range(ends)]),
                cells,
                lax.ppermute(head, axis, [((i + 1) % count, i) for i in range(ends)]),
            ],
            axis=dim,
        )
    return cells


def conv_taps(padded, height, width, dw_kernel):
    mixed = jnp.zeros((height, width, padded.shape[2]), jnp.float32)
    for row_tap in range(7):
        for col_tap in range(7):
            mixed = (
                mixed
                + padded[row_tap : row_tap + height, col_tap : col_tap + width]
                * dw_kernel[row_tap, col_tap]
            )
    return mixed


def layer_norm(mixed, norm_gain, norm_shift):
    center = mixed - jnp.mean(mixed, axis=-1, keepdims=True)
    spread = jnp.mean(center * center, axis=-1, keepdims=True)
    return (center * lax.rsqrt(spread + 1e-06) * norm_gain + norm_shift).astype(jnp.bfloat16)


def finish_latents(numer, denom, latent_gain, w_full):
    attended = (numer / denom[..., None]).reshape(numer.shape[0], -1)
    squares = jnp.mean(attended * attended, axis=-1, keepdims=True)
    scaled = (attended * lax.rsqrt(squares + 1e-06) * latent_gain).astype(jnp.bfloat16)
    return jnp.dot(scaled, w_full, preferred_element_type=jnp.float32).astype(jnp.bfloat16)


def body(tokens, dw_kernel, norm_gain, norm_shift, w_in, w_out, w_kv, queries, latent_gain, w_o):
    height, width, width_d = tokens.shape
    latent_count = queries.shape[0]
    padded = with_halo(tokens, (("row", 0), ("col", 1)), 3)
    mixed = conv_taps(padded.astype(jnp.float32), height, width, dw_kernel)
    normed = layer_norm(mixed, norm_gain, norm_shift).reshape(height * width, width_d)
    residual = tokens.reshape(height * width, width_d).astype(jnp.float32)
    hidden = jax.nn.gelu(
        jnp.dot(
            normed,
            lax.all_gather(w_in, "col", axis=1, tiled=True),
            preferred_element_type=jnp.float32,
        )
    ).astype(jnp.bfloat16)
    update = jnp.dot(
        hidden, lax.all_gather(w_out, "col", axis=0, tiled=True), preferred_element_type=jnp.float32
    )
    token_rows = (residual + update).astype(jnp.bfloat16)
    token_map = token_rows.reshape(height, width, width_d)
    keys_vals = jnp.dot(
        token_rows,
        lax.all_gather(w_kv, "col", axis=1, tiled=True),
        preferred_element_type=jnp.float32,
    ).astype(jnp.bfloat16)
    w_full = lax.all_gather(w_o, "col", axis=1, tiled=True)
    key_heads = keys_vals[:, :width_d].reshape(-1, HEADS, HEAD)
    val_heads = keys_vals[:, width_d:].reshape(-1, HEADS, HEAD)
    query_heads = queries.reshape(latent_count, HEADS, HEAD)
    score_scale = 1.0 / math.sqrt(HEAD)
    group_size = math.gcd(HEADS, 4)
    max_parts, den_parts, num_parts = ([], [], [])
    for first_head in range(0, HEADS, group_size):
        scores = (
            jnp.einsum(
                "lhd,thd->lht",
                query_heads[:, first_head : first_head + group_size],
                key_heads[:, first_head : first_head + group_size],
                preferred_element_type=jnp.float32,
            )
            * score_scale
        )
        local_max = jnp.max(scores, axis=-1)
        weights = jnp.exp(scores - local_max[..., None])
        den_parts.append(jnp.sum(weights, axis=-1))
        max_parts.append(local_max)
        num_parts.append(
            jnp.einsum(
                "lht,thd->lhd",
                weights.astype(jnp.bfloat16),
                val_heads[:, first_head : first_head + group_size],
                preferred_element_type=jnp.float32,
            )
        )
    maxima = jnp.concatenate(max_parts, axis=1)
    denom = jnp.concatenate(den_parts, axis=1)
    numer = jnp.concatenate(num_parts, axis=1)
    peak = lax.pmax(maxima, ("row", "col"))
    factor = jnp.exp(maxima - peak)
    den_terms = denom * factor
    num_terms = (numer * factor[..., None]).reshape(latent_count, width_d)
    den_part, num_part = (
        lax.psum_scatter(den_terms, "col", scatter_dimension=0, tiled=True),
        lax.psum_scatter(num_terms, "col", scatter_dimension=0, tiled=True),
    )
    den_share, num_share = lax.psum((den_part, num_part), "row")
    own_rows = finish_latents(
        num_share.reshape(num_share.shape[0], HEADS, HEAD), den_share, latent_gain, w_full
    )
    latents = lax.all_gather(own_rows, "col", axis=0, tiled=True)
    return (token_map, latents)


def solution(mesh):
    in_specs = (
        P("row", "col", None),
        P(),
        P(),
        P(),
        P(None, "col"),
        P("col", None),
        P(None, "col"),
        P(),
        P(),
        P(None, "col"),
    )
    out_specs = (P("row", "col", None), P())
    return jax.shard_map(kernel_body, mesh=mesh, in_specs=in_specs, out_specs=out_specs, check_vma=False)
```

```python
import functools
import math

import jax
import jax.numpy as jnp
from jax import lax
from jax.experimental import pallas as pl
from jax.experimental.pallas import tpu as pltpu
from jax.sharding import PartitionSpec as P

HEADS = 12
HEAD = 64
HALO = 3
EDGE = 8
LANES = 128
MESH = pl.DeviceIdType.MESH
VMEM_BYTES = 60 * 1024 * 1024


def log2(count):
    return count.bit_length() - 1


def barrier_with(peers):
    barrier = pltpu.get_barrier_semaphore()
    total = 0
    for cond, device in peers:
        if cond is None:
            pl.semaphore_signal(barrier, inc=1, device_id=device, device_id_type=MESH)
            total = total + 1
        else:

            @pl.when(cond)
            def _():
                pl.semaphore_signal(barrier, inc=1, device_id=device, device_id_type=MESH)

            total = total + jnp.where(cond, 1, 0)
    pl.semaphore_wait(barrier, total)


def block_kernel(
    rows,
    cols,
    tokens,
    dw,
    gain,
    shift,
    w_in,
    w_out,
    w_kv,
    w_o,
    queries,
    tok_out,
    num_out,
    stat_out,
    wo_out,
    g_in,
    g_out,
    g_kv,
    pad,
    mixed,
    normed,
    hidden,
    acc,
    tok_bf,
    kv,
    h_rows,
    h_cols,
    h_corners,
    halo_send,
    halo_recv,
    send_sem,
    recv_sem,
    pass_send,
    pass_recv,
    local_sem,
):
    bits = log2(rows)
    row, col = lax.axis_index("row"), lax.axis_index("col")
    height, width, depth = tokens.shape
    count = height * width
    coords = [(row // (1 << (bits - 1 - i))) % 2 for i in range(bits)]

    def partner(dim):
        step = 1 << (bits - 1 - dim)
        return row + step * (1 - 2 * coords[dim])

    halo = []
    for dr in (-1, 0, 1):
        for dc in (-1, 0, 1):
            if dr == 0 and dc == 0:
                continue
            cond = None
            for d, pos, n in ((dr, row, rows), (dc, col, cols)):
                if d:
                    one = (pos + d >= 0) & (pos + d < n)
                    cond = one if cond is None else cond & one
            halo.append((dr, dc, cond))

    peers = [(cond, (row + dr, col + dc)) for dr, dc, cond in halo]
    peers += [(None, (row, (col + j) % cols)) for j in range(1, cols)]
    peers += [(None, (partner(i), col)) for i in range(bits)]
    barrier_with(peers)

    def halo_slot(dr, dc):
        if dc == 0:
            return h_rows.at[0 if dr < 0 else 1]
        if dr == 0:
            return h_cols.at[0 if dc < 0 else 1]
        return h_corners.at[(0 if dr < 0 else 2) + (0 if dc < 0 else 1)]

    def halo_copy(i, dr, dc):
        r_span = {-1: pl.ds(0, HALO), 0: slice(None), 1: pl.ds(height - HALO, HALO)}[dr]
        c_span = {-1: pl.ds(0, EDGE), 0: slice(None), 1: pl.ds(width - EDGE, EDGE)}[dc]
        src = tokens.at[r_span, c_span]
        return pltpu.make_async_remote_copy(
            src_ref=src,
            dst_ref=halo_slot(-dr, -dc),
            send_sem=halo_send.at[i],
            recv_sem=halo_recv.at[len(halo) - 1 - i],
            device_id=(row + dr, col + dc),
            device_id_type=MESH,
        )

    for i, (dr, dc, cond) in enumerate(halo):

        @pl.when(cond)
        def _():
            halo_copy(i, dr, dc).start()

    shards = (w_in, w_out, w_kv, w_o)
    fulls = (g_in, g_out, g_kv, wo_out)
    own = tuple(coords)
    units = [(w, k) for w in range(4) for k in range(cols - 1)]

    def rank(c, side, d):
        both = jnp.minimum(c, cols - 1 - c)
        return jnp.where(d <= both, 2 * (d - 1) + (0 if side > 0 else 1), d - 1 + both)

    both = jnp.minimum(col, cols - 1 - col)
    longer = jnp.where(cols - 1 - col > col, 1, -1)
    sides, gaps, blocks = [], [], []
    for k in range(cols - 1):
        paired = k < 2 * both
        sides.append(jnp.where(paired, 1 - 2 * (k % 2), longer))
        gaps.append(jnp.where(paired, k // 2 + 1, k - both + 1))
        blocks.append(col + sides[k] * gaps[k])

    def pass_on(w, k, side):
        to = col - side
        block = col if k is None else blocks[k]
        gap = 1 if k is None else gaps[k] + 1
        src = shards[w].at[own] if k is None else fulls[w].at[(block,) + own]
        cond = (to >= 0) & (to < cols)
        if k is not None:
            cond = cond & (sides[k] == side)
        place = (cols - 1 + (0 if side > 0 else 1)) if k is None else k
        unit = w * (cols - 1) + rank(to, side, gap)
        return cond, pltpu.make_async_remote_copy(
            src_ref=src,
            dst_ref=fulls[w].at[(block,) + own],
            send_sem=pass_send.at[w * (cols + 1) + place],
            recv_sem=pass_recv.at[unit],
            device_id=(row, to),
            device_id_type=MESH,
        )

    def each_pass(w, k, act):
        for side in (1, -1):
            cond, c = pass_on(w, k, side)

            @pl.when(cond)
            def _():
                act(c)

    halves = [len(w.shape) - bits - 2 for w in shards]
    ways = bits + (bits - 1) + 1

    def unit_copies(u, phase):
        w, k = units[u]
        slot = u * ways
        if phase == 0:
            ref = fulls[w].at[(blocks[k],) + own]
            return [pltpu.make_async_copy(ref, ref, pass_recv.at[u])]
        else:
            block = blocks[k]
            split = halves[w] and phase < bits
            trips = []
            for half in range(2 if split else 1):
                order = list(range(bits - 1))
                if (half if split else u % 2):
                    order = order[::-1]
                order = order + [bits - 1]
                done = order[: phase - 1]
                idx = (block,) + tuple(slice(None) if i in done else own[i] for i in range(bits))
                if split:
                    idx = idx + (half,)
                ref = fulls[w].at[idx]
                at = slot + ways - 1 if phase == bits else slot + 1 + 2 * (phase - 1) + half
                trips.append((ref, ref, (partner(order[phase - 1]), col), at))
        return [
            pltpu.make_async_remote_copy(
                src_ref=src,
                dst_ref=dst,
                send_sem=send_sem.at[at],
                recv_sem=recv_sem.at[at],
                device_id=target,
                device_id_type=MESH,
            )
            for src, dst, target, at in trips
        ]

    for w in range(4):
        each_pass(w, None, lambda c: c.start())
    local = []
    for w in range(4):
        copy = pltpu.make_async_copy(shards[w], fulls[w].at[col], local_sem.at[w])
        copy.start()
        local.append(copy)

    lag = 2
    state = {"tick": 0}
    ticks = len(units) + lag * bits

    def tick():
        t = state["tick"]
        if t >= ticks:
            return
        state["tick"] = t + 1
        for phase in range(bits, -1, -1):
            u = t - lag * phase
            if 0 <= u < len(units):
                for c in unit_copies(u, phase):
                    c.wait() if phase == 0 else c.wait_recv()
                if phase == 0:
                    each_pass(*units[u], lambda c: c.start())
                if phase < bits:
                    for c in unit_copies(u, phase + 1):
                        c.start()

    def finish_unit(u):
        while state["tick"] <= u + lag * bits:
            tick()

    pad[pl.ds(HALO, height), pl.ds(EDGE, width), :] = tokens[...].astype(jnp.float32)
    spans = {-1: (0, HALO), 0: (HALO, height), 1: (HALO + height, HALO)}
    lanes_of = {-1: (0, EDGE), 0: (EDGE, width), 1: (EDGE + width, EDGE)}
    for i, (dr, dc, cond) in enumerate(halo):
        r0, rn = spans[dr]
        c0, cn = lanes_of[dc]

        @pl.when(cond)
        def _():
            halo_copy(len(halo) - 1 - i, -dr, -dc).wait_recv()
            pad[pl.ds(r0, rn), pl.ds(c0, cn), :] = halo_slot(dr, dc)[...].astype(jnp.float32)

        @pl.when(jnp.logical_not(cond))
        def _():
            pad[pl.ds(r0, rn), pl.ds(c0, cn), :] = jnp.zeros((rn, cn, depth), jnp.float32)

    taps = 2 * HALO + 1
    chunks = depth // LANES

    def conv_rows(first, n_rows):
        def one(step, carry):
            i = first + step // chunks
            q = pl.multiple_of((step % chunks) * LANES, LANES)
            sums = [None] * taps
            for a in range(taps):
                line = pad[i + a, :, pl.ds(q, LANES)]
                for b in range(taps):
                    lo = 0 if b < HALO else EDGE
                    hi = EDGE + width + (EDGE if b > HALO else 0)
                    term = line[lo:hi] * dw[a, pl.ds(b, 1), pl.ds(q, LANES)]
                    sums[b] = term if sums[b] is None else sums[b] + term
            total = sums[HALO]
            for b in range(taps):
                if b == HALO:
                    continue
                size = width + EDGE
                offset = EDGE - HALO + b - (0 if b < HALO else EDGE)
                total = total + pltpu.roll(sums[b], (size - offset) % size, 0)[:width]
            mixed[i, :, pl.ds(q, LANES)] = total
            return carry

        lax.fori_loop(0, n_rows * chunks, one, 0)

    group = 2
    span = group * width

    def norm_rows(g, carry):
        value = mixed[pl.ds(g * group, group), :, :].reshape(span, depth)
        center = value - jnp.mean(value, axis=-1, keepdims=True)
        spread = jnp.mean(center * center, axis=-1, keepdims=True)
        out = center * lax.rsqrt(spread + 1e-06) * gain[...][None, :] + shift[...][None, :]
        normed[pl.ds(pl.multiple_of(g * span, 16), span), :] = out.astype(jnp.bfloat16)
        return carry

    quarter = height // 4
    for part in range(4):
        conv_rows(part * quarter, quarter)
        tick()
    lax.fori_loop(0, height // group, norm_rows, 0)
    for copy in local:
        copy.wait()

    def wide(ref, block, lo, size):
        value = ref[(block,) + (slice(None),) * (bits + 2) + (pl.ds(lo, size),)]
        return value.reshape(-1, size)

    f_width = w_in.shape[-1]
    tile = 256 if f_width % 256 == 0 else LANES

    def expand(block):
        def one(n, carry):
            lo = pl.multiple_of(n * tile, tile)
            u = jnp.dot(normed[...], wide(g_in, block, lo, tile), preferred_element_type=jnp.float32)
            hidden[block, :, pl.ds(lo, tile)] = jax.nn.gelu(u).astype(jnp.bfloat16)
            return carry

        lax.fori_loop(0, f_width // tile, one, 0)

    def contract(block, fresh):
        def one(n, carry):
            lo = pl.multiple_of(n * 256, 256)
            part = jnp.dot(
                hidden[block], wide(g_out, block, lo, 256), preferred_element_type=jnp.float32
            )
            if fresh:
                acc[:, pl.ds(lo, 256)] = part
            else:
                acc[:, pl.ds(lo, 256)] += part
            return carry

        lax.fori_loop(0, depth // 256, one, 0)

    expand(col)
    tick()
    contract(col, True)
    for j in range(1, cols):
        finish_unit(j - 1)
        expand(blocks[j - 1])
    for j in range(1, cols):
        finish_unit(cols - 1 + j - 1)
        contract(blocks[j - 1], False)

    def close_rows(g, carry):
        base = pad[pl.ds(HALO + g * group, group), pl.ds(EDGE, width), :].reshape(span, depth)
        at = pl.ds(pl.multiple_of(g * span, 16), span)
        total = base + acc[at, :]
        tok_out[pl.ds(g * group, group), :, :] = total.reshape(group, width, depth).astype(jnp.bfloat16)
        tok_bf[at, :] = total.astype(jnp.bfloat16)
        return carry

    lax.fori_loop(0, height // group, close_rows, 0)

    kv_width = w_kv.shape[-1]

    def project(block):
        def one(n, carry):
            lo = pl.multiple_of(n * LANES, LANES)
            out = jnp.dot(tok_bf[...], wide(g_kv, block, lo, LANES), preferred_element_type=jnp.float32)
            kv[block, :, pl.ds(lo, LANES)] = out.astype(jnp.bfloat16)
            return carry

        lax.fori_loop(0, kv_width // LANES, one, 0)

    project(col)
    for j in range(1, cols):
        finish_unit(2 * (cols - 1) + j - 1)
        project(blocks[j - 1])

    latents = queries.shape[0]
    scale = 1.0 / math.sqrt(HEAD)
    stat_out[...] = jnp.zeros((latents, LANES), jnp.float32)
    side = lax.broadcasted_iota(jnp.int32, (1, LANES), 1)

    def attend(pair, carry):
        at = pl.multiple_of(pair * LANES, LANES)
        k_at, v_at = at, depth + at
        keys = kv[k_at // kv_width, :, pl.ds(pl.multiple_of(k_at % kv_width, LANES), LANES)]
        vals = kv[v_at // kv_width, :, pl.ds(pl.multiple_of(v_at % kv_width, LANES), LANES)]
        q = queries[:, pl.ds(at, LANES)]
        stat = stat_out[...]
        outs = []
        for s in range(2):
            keep = (side // HEAD) == s
            q_one = jnp.where(keep, q, jnp.zeros_like(q))
            scores = lax.dot_general(
                q_one, keys, (((1,), (1,)), ((), ())), preferred_element_type=jnp.float32
            )
            top = jnp.max(scores, axis=-1, keepdims=True)
            weights = jnp.exp((scores - top) * scale)
            den = jnp.sum(weights, axis=-1, keepdims=True)
            outs.append(
                jnp.dot(weights.astype(jnp.bfloat16), vals, preferred_element_type=jnp.float32)
            )
            lane = pair * 2 + s
            stat = jnp.where(side == lane, top * scale, stat)
            stat = jnp.where(side == lane + HEAD, den, stat)
        stat_out[...] = stat
        num_out[:, pl.ds(at, LANES)] = jnp.where(side < HEAD, outs[0], outs[1]).astype(jnp.bfloat16)
        return carry

    lax.fori_loop(0, depth // LANES, attend, 0)

    finish_unit(len(units) - 1)
    for i, (dr, dc, cond) in enumerate(halo):

        @pl.when(cond)
        def _():
            halo_copy(i, dr, dc).wait_send()

    for u in range(len(units)):
        each_pass(*units[u], lambda c: c.wait_send())
        for phase in range(1, bits + 1):
            for c in unit_copies(u, phase):
                c.wait_send()
    for w in range(4):
        each_pass(w, None, lambda c: c.wait_send())


def per_head(factors, n):
    side = lax.broadcasted_iota(jnp.int32, (1, LANES), 1)
    parts = []
    for pair in range(HEADS // 2):
        lo = jnp.broadcast_to(factors[:, 2 * pair : 2 * pair + 1], (n, LANES))
        hi = jnp.broadcast_to(factors[:, 2 * pair + 1 : 2 * pair + 2], (n, LANES))
        parts.append(jnp.where(side < HEAD, lo, hi))
    return jnp.concatenate(parts, axis=-1)


def merge(stats, nums):
    n = stats[0].shape[0]
    side = lax.broadcasted_iota(jnp.int32, (1, LANES), 1)
    peak = functools.reduce(jnp.maximum, stats)
    den, num = None, None
    for stat, part in zip(stats, nums):
        factor = jnp.exp(stat - peak)
        d = pltpu.roll(stat, HEAD, 1) * factor
        t = part.astype(jnp.float32) * per_head(factor, n)
        den = d if den is None else den + d
        num = t if num is None else num + t
    return jnp.where(side < HEAD, peak, pltpu.roll(den, HEAD, 1)), num


def latent_kernel(
    rows, cols, num_in, stat_in, latent_gain, out, num, stat, got_num, got_stat, send_sem, recv_sem
):
    bits = log2(rows)
    row, col = lax.axis_index("row"), lax.axis_index("col")
    latents = num_in.shape[0]

    def bit(i):
        return (row // (1 << i)) % 2

    def partner(i):
        return row + (1 << i) * (1 - 2 * bit(i))

    peers = [(None, (row, (col + j) % cols)) for j in range(1, cols)]
    peers += [(None, (partner(i), col)) for i in range(bits)]
    barrier_with(peers)

    def copy(src, dst, slot, device):
        return pltpu.make_async_remote_copy(
            src_ref=src,
            dst_ref=dst,
            send_sem=send_sem.at[slot],
            recv_sem=recv_sem.at[slot],
            device_id=device,
            device_id_type=MESH,
        )

    sent = []
    slots = iter(range(4 * bits + 3 * (cols - 1) + 2 * bits))
    rest = list(range(1, bits))
    orders = [[0] + rest, [0] + rest[::-1]]
    held = [[], []]
    offset = 0
    trips = {}

    def exchange(s, p):
        nonlocal offset
        i = orders[s][p]
        if p == 0:
            size = latents // 4
            mine = bit(i) * 2 * size + s * size
            theirs = (1 - bit(i)) * 2 * size + s * size
        else:
            base, whole = held[s][-1]
            size = whole // 2
            mine, theirs = base + bit(i) * size, base + (1 - bit(i)) * size
        src_num, src_stat = (num_in, stat_in) if p == 0 else (num, stat)
        give = pl.ds(pl.multiple_of(theirs, 16), size)
        land = pl.ds(offset, size)
        pair = [
            copy(src_stat.at[give], got_stat.at[land], next(slots), (partner(i), col)),
            copy(src_num.at[give], got_num.at[land], next(slots), (partner(i), col)),
        ]
        for c in pair:
            c.start()
        trips[s, p] = (pair, offset)
        held[s].append((mine, size))
        offset = offset + size

    def collect(s, p):
        pair, first = trips[s, p]
        for c in pair:
            c.wait_recv()
        sent.extend(pair)
        mine, size = held[s][p]
        src_num, src_stat = (num_in, stat_in) if p == 0 else (num, stat)
        step = min(size, 32)

        def fold(k, carry):
            at = pl.ds(pl.multiple_of(mine + k * step, 16), step)
            came = pl.ds(pl.multiple_of(first + k * step, 16), step)
            new_stat, new_num = merge(
                [src_stat[at, :], got_stat[came, :]], [src_num[at, :], got_num[came, :]]
            )
            stat[at, :] = new_stat
            num[at, :] = new_num.astype(jnp.bfloat16)
            return carry

        lax.fori_loop(0, size // step, fold, 0)

    for s in range(2):
        exchange(s, 0)
    for p in range(bits):
        for s in range(2):
            collect(s, p)
            if p + 1 < bits:
                exchange(s, p + 1)

    share = latents // (rows * cols)
    side_cols = cols // 2

    def chunk(c):
        base = jnp.where(
            c < side_cols, held[0][-1][0] + c * share, held[1][-1][0] + (c - side_cols) * share
        )
        return pl.ds(pl.multiple_of(base, 16), share)

    arrived = []
    for j in range(1, cols):
        other = (col + cols - j) % cols
        land = pl.ds(offset + (j - 1) * share, share)
        pair = [
            copy(stat.at[chunk(other)], got_stat.at[land], next(slots), (row, other)),
            copy(num.at[chunk(other)], got_num.at[land], next(slots), (row, other)),
        ]
        for c in pair:
            c.start()
        sent += pair
        arrived.append((pair, land))
    for pair, _ in arrived:
        for c in pair:
            c.wait_recv()
    own = chunk(col)
    final_stat, final_num = merge(
        [stat[own, :]] + [got_stat[land, :] for _, land in arrived],
        [num[own, :]] + [got_num[land, :] for _, land in arrived],
    )
    attended = final_num / per_head(pltpu.roll(final_stat, HEAD, 1), share)
    squares = jnp.mean(attended * attended, axis=-1, keepdims=True)
    scaled = attended * lax.rsqrt(squares + 1e-06) * latent_gain[...][None, :]
    out[own, :] = scaled.astype(jnp.bfloat16)

    gather = []
    for j in range(1, cols):
        c = copy(out.at[own], out.at[own], next(slots), (row, (col + cols - j) % cols))
        c.start()
        gather.append(c)
    for c in gather:
        c.wait_recv()
    sent += gather
    back = [None, None]
    for p in reversed(range(bits)):
        for s in range(2):
            if back[s] is not None:
                back[s].wait_recv()
            base, size = held[s][p]
            rows_held = pl.ds(pl.multiple_of(base, 16), size)
            back[s] = copy(
                out.at[rows_held], out.at[rows_held], next(slots), (partner(orders[s][p]), col)
            )
            back[s].start()
            sent.append(back[s])
    for s in range(2):
        back[s].wait_recv()
    for c in sent:
        c.wait_send()


def vmem(n):
    return [pl.BlockSpec(memory_space=pltpu.VMEM)] * n


def fits(mesh_rows, mesh_cols, tokens, w_in, w_kv, queries):
    height, width, depth = tokens.shape
    return (
        mesh_rows >= 2
        and mesh_cols >= 2
        and mesh_cols % 2 == 0
        and mesh_rows & (mesh_rows - 1) == 0
        and depth % (32 * mesh_rows) == 0
        and w_in.shape[1] % LANES == 0
        and w_in.shape[1] % (32 * mesh_rows) == 0
        and depth // mesh_cols % (8 * mesh_rows) == 0
        and w_kv.shape[1] % LANES == 0
        and queries.shape[0] % (16 * mesh_rows * mesh_cols) == 0
        and depth % 256 == 0
        and height % 4 == 0
        and width % 8 == 0
        and 2 * width % 16 == 0
    )


def kernel_body(tokens, dw_kernel, norm_gain, norm_shift, w_in, w_out, w_kv, queries, latent_gain, w_o):
    rows, cols = lax.axis_size("row"), lax.axis_size("col")
    height, width, depth = tokens.shape
    if not fits(rows, cols, tokens, w_in, w_kv, queries):
        return body(
            tokens, dw_kernel, norm_gain, norm_shift, w_in, w_out, w_kv, queries, latent_gain, w_o
        )
    bits = log2(rows)
    count = height * width
    latents = queries.shape[0]
    f_width = w_in.shape[1]
    grid = (2,) * bits
    bf16, f32 = jnp.bfloat16, jnp.float32

    def cut(w, parts):
        tail = (2, w.shape[0] // rows // 2) if parts == 2 else (w.shape[0] // rows,)
        return w.reshape(grid + tail + (w.shape[1],))

    shards = [cut(w_in, 2), cut(w_out, 2), cut(w_kv, 2), cut(w_o.T, 1)]
    units = 4 * (cols - 1)
    token_map, num, stat, wo_full = pl.pallas_call(
        functools.partial(block_kernel, rows, cols),
        out_shape=(
            jax.ShapeDtypeStruct(tokens.shape, bf16),
            jax.ShapeDtypeStruct((latents, depth), bf16),
            jax.ShapeDtypeStruct((latents, LANES), f32),
            jax.ShapeDtypeStruct((cols,) + shards[3].shape, bf16),
        ),
        in_specs=vmem(9),
        out_specs=tuple(vmem(4)),
        scratch_shapes=[
            pltpu.VMEM((cols,) + shards[0].shape, bf16),
            pltpu.VMEM((cols,) + shards[1].shape, bf16),
            pltpu.VMEM((cols,) + shards[2].shape, bf16),
            pltpu.VMEM((height + 2 * HALO, width + 2 * EDGE, depth), f32),
            pltpu.VMEM((height, width, depth), f32),
            pltpu.VMEM((count, depth), bf16),
            pltpu.VMEM((cols, count, f_width), bf16),
            pltpu.VMEM((count, depth), f32),
            pltpu.VMEM((count, depth), bf16),
            pltpu.VMEM((cols, count, w_kv.shape[1]), bf16),
            pltpu.VMEM((2, HALO, width, depth), bf16),
            pltpu.VMEM((2, height, EDGE, depth), bf16),
            pltpu.VMEM((4, HALO, EDGE, depth), bf16),
            pltpu.SemaphoreType.DMA((8,)),
            pltpu.SemaphoreType.DMA((8,)),
            pltpu.SemaphoreType.DMA((units * 2 * bits,)),
            pltpu.SemaphoreType.DMA((units * 2 * bits,)),
            pltpu.SemaphoreType.DMA((4 * (cols + 1),)),
            pltpu.SemaphoreType.DMA((units,)),
            pltpu.SemaphoreType.DMA((4,)),
        ],
        compiler_params=pltpu.CompilerParams(
            collective_id=0, has_side_effects=True, vmem_limit_bytes=VMEM_BYTES
        ),
        name="block",
    )(
        tokens,
        dw_kernel,
        norm_gain,
        norm_shift,
        *shards,
        queries,
    )
    slots = 4 * bits + 3 * (cols - 1) + 2 * bits
    scaled = pl.pallas_call(
        functools.partial(latent_kernel, rows, cols),
        out_shape=jax.ShapeDtypeStruct((latents, depth), bf16),
        in_specs=vmem(3),
        out_specs=vmem(1)[0],
        scratch_shapes=[
            pltpu.VMEM((latents, depth), bf16),
            pltpu.VMEM((latents, LANES), f32),
            pltpu.VMEM((latents, depth), bf16),
            pltpu.VMEM((latents, LANES), f32),
            pltpu.SemaphoreType.DMA((slots,)),
            pltpu.SemaphoreType.DMA((slots,)),
        ],
        compiler_params=pltpu.CompilerParams(
            collective_id=1, has_side_effects=True, vmem_limit_bytes=VMEM_BYTES
        ),
        name="latents",
    )(num, stat, latent_gain)
    w_turned = wo_full.reshape(-1, depth)
    latents_out = lax.dot_general(
        scaled, w_turned, (((1,), (1,)), ((), ())), preferred_element_type=f32
    ).astype(bf16)
    return (token_map, latents_out)


def with_halo(cells, sides, width):
    for axis, dim in sides:
        count = lax.axis_size(axis)
        ends = count - 1
        head = lax.slice_in_dim(cells, 0, width, axis=dim)
        tail = lax.slice_in_dim(cells, cells.shape[dim] - width, cells.shape[dim], axis=dim)
        cells = jnp.concatenate(
            [
                lax.ppermute(tail, axis, [(i, (i + 1) % count) for i in range(ends)]),
                cells,
                lax.ppermute(head, axis, [((i + 1) % count, i) for i in range(ends)]),
            ],
            axis=dim,
        )
    return cells


def conv_taps(padded, height, width, dw_kernel):
    mixed = jnp.zeros((height, width, padded.shape[2]), jnp.float32)
    for row_tap in range(7):
        for col_tap in range(7):
            mixed = (
                mixed
                + padded[row_tap : row_tap + height, col_tap : col_tap + width]
                * dw_kernel[row_tap, col_tap]
            )
    return mixed


def layer_norm(mixed, norm_gain, norm_shift):
    center = mixed - jnp.mean(mixed, axis=-1, keepdims=True)
    spread = jnp.mean(center * center, axis=-1, keepdims=True)
    return (center * lax.rsqrt(spread + 1e-06) * norm_gain + norm_shift).astype(jnp.bfloat16)


def finish_latents(numer, denom, latent_gain, w_full):
    attended = (numer / denom[..., None]).reshape(numer.shape[0], -1)
    squares = jnp.mean(attended * attended, axis=-1, keepdims=True)
    scaled = (attended * lax.rsqrt(squares + 1e-06) * latent_gain).astype(jnp.bfloat16)
    return jnp.dot(scaled, w_full, preferred_element_type=jnp.float32).astype(jnp.bfloat16)


def body(tokens, dw_kernel, norm_gain, norm_shift, w_in, w_out, w_kv, queries, latent_gain, w_o):
    height, width, width_d = tokens.shape
    latent_count = queries.shape[0]
    padded = with_halo(tokens, (("row", 0), ("col", 1)), 3)
    mixed = conv_taps(padded.astype(jnp.float32), height, width, dw_kernel)
    normed = layer_norm(mixed, norm_gain, norm_shift).reshape(height * width, width_d)
    residual = tokens.reshape(height * width, width_d).astype(jnp.float32)
    hidden = jax.nn.gelu(
        jnp.dot(
            normed,
            lax.all_gather(w_in, "col", axis=1, tiled=True),
            preferred_element_type=jnp.float32,
        )
    ).astype(jnp.bfloat16)
    update = jnp.dot(
        hidden, lax.all_gather(w_out, "col", axis=0, tiled=True), preferred_element_type=jnp.float32
    )
    token_rows = (residual + update).astype(jnp.bfloat16)
    token_map = token_rows.reshape(height, width, width_d)
    keys_vals = jnp.dot(
        token_rows,
        lax.all_gather(w_kv, "col", axis=1, tiled=True),
        preferred_element_type=jnp.float32,
    ).astype(jnp.bfloat16)
    w_full = lax.all_gather(w_o, "col", axis=1, tiled=True)
    key_heads = keys_vals[:, :width_d].reshape(-1, HEADS, HEAD)
    val_heads = keys_vals[:, width_d:].reshape(-1, HEADS, HEAD)
    query_heads = queries.reshape(latent_count, HEADS, HEAD)
    score_scale = 1.0 / math.sqrt(HEAD)
    group_size = math.gcd(HEADS, 4)
    max_parts, den_parts, num_parts = ([], [], [])
    for first_head in range(0, HEADS, group_size):
        scores = (
            jnp.einsum(
                "lhd,thd->lht",
                query_heads[:, first_head : first_head + group_size],
                key_heads[:, first_head : first_head + group_size],
                preferred_element_type=jnp.float32,
            )
            * score_scale
        )
        local_max = jnp.max(scores, axis=-1)
        weights = jnp.exp(scores - local_max[..., None])
        den_parts.append(jnp.sum(weights, axis=-1))
        max_parts.append(local_max)
        num_parts.append(
            jnp.einsum(
                "lht,thd->lhd",
                weights.astype(jnp.bfloat16),
                val_heads[:, first_head : first_head + group_size],
                preferred_element_type=jnp.float32,
            )
        )
    maxima = jnp.concatenate(max_parts, axis=1)
    denom = jnp.concatenate(den_parts, axis=1)
    numer = jnp.concatenate(num_parts, axis=1)
    peak = lax.pmax(maxima, ("row", "col"))
    factor = jnp.exp(maxima - peak)
    den_terms = denom * factor
    num_terms = (numer * factor[..., None]).reshape(latent_count, width_d)
    den_part, num_part = (
        lax.psum_scatter(den_terms, "col", scatter_dimension=0, tiled=True),
        lax.psum_scatter(num_terms, "col", scatter_dimension=0, tiled=True),
    )
    den_share, num_share = lax.psum((den_part, num_part), "row")
    own_rows = finish_latents(
        num_share.reshape(num_share.shape[0], HEADS, HEAD), den_share, latent_gain, w_full
    )
    latents = lax.all_gather(own_rows, "col", axis=0, tiled=True)
    return (token_map, latents)


def solution(mesh):
    in_specs = (
        P("row", "col", None),
        P(),
        P(),
        P(),
        P(None, "col"),
        P("col", None),
        P(None, "col"),
        P(),
        P(),
        P(None, "col"),
    )
    out_specs = (P("row", "col", None), P())
    return jax.shard_map(kernel_body, mesh=mesh, in_specs=in_specs, out_specs=out_specs, check_vma=False)
```
